32 devices in a mesh: grp: 2 (over y), tile: 16 (over z, x, core).
Axes of the slice: x: 2, y: 2, z: 4, core: 2. Of those that a mesh axis runs over, the one named last changes fastest.
Arguments:
- fields: bfloat16 [6, 128, 128, 256], P('grp', 'tile'), parts along dimension 0, may hold values from -6 to 6
- seam_tile: int32 [3, 16, 2], P(None, 'tile'), may hold values from 0 to 47, as said below
- seam_code: int32 [3, 16, 2], P(None, 'tile'), may hold values from 0 to 3
- encoder_weight: bfloat16 [3, 3, 256, 256], replicated, may hold values from -0.125 to 0.125
- encoder_bias: float32 [256], replicated, may hold values from -3 to 3
- middle_weight: bfloat16 [3, 3, 256, 256], replicated, may hold values from -0.125 to 0.125
- middle_bias: float32 [256], replicated, may hold values from -3 to 3
- upconv_weight: bfloat16 [2, 2, 256, 256], replicated, may hold values from -0.375 to 0.375
- upconv_bias: float32 [256], replicated, may hold values from -3 to 3
- decoder_weight: bfloat16 [3, 3, 512, 256], replicated, may hold values from -0.09375 to 0.09375
- decoder_offset_bias: float32 [256], replicated, may hold values from -3 to 3
Outputs:
- decoded: bfloat16 [6, 128, 128, 256], P('grp', 'tile'), parts along dimension 0
The draws below stay inside these ranges and needn't reach their ends.
There are 2 independent parts, one for each index of `grp`. The reference program is written for one: setup_inputs(seed, part) draws one part's arguments, and reference() takes and returns one part's arrays. A program takes and returns all parts, laid end to end along the dimension named above; an argument that names none is the same for every part. Nothing has to cross between parts.
Inputs may be any that keep to these rules, and one draw needn't show every extreme that they name: `seam_tile`: for each side, the 12 faces (cycle, face) name 12 different partner faces; all 4 tiles of one face side share the partner face and the code, and strip s names the tile of strip s of the partner face, or of strip 4 - 1 - s where the code is 2 or more.
All inputs are finite; a program needn't handle non-finite values.
Results may differ from the reference program's by a relative error of at most 0.0048.
Values may be sent and summed in bfloat16 or wider, within the bound.
A program may use at most 128 MiB of HBM per device.

```python
import jax
import jax.numpy as jnp

C = 256
COLS = 128
TILES = 16
STRIPS = 4
ROWS = 128


def seam_layout(key):
    base = jax.random.fold_in(key, 7)
    key_left, key_right, key_code = jax.random.split(base, 3)
    order_left = jax.random.permutation(key_left, 12)
    order_right = jax.random.permutation(key_right, 12)
    partner_face = jnp.stack([order_left, order_right], axis=-1).reshape(3, 4, 1, 2).astype(jnp.int32)
    code_order = jax.random.permutation(key_code, 24)
    face_code = (code_order % 4).reshape(3, 4, 1, 2).astype(jnp.int32)
    strip_index = jnp.arange(STRIPS, dtype=jnp.int32).reshape(1, 1, STRIPS, 1)
    partner_strip = jnp.where(face_code >= 2, STRIPS - 1 - strip_index, strip_index)
    partner_cycle = partner_face // 4
    partner_in_cycle = partner_face % 4
    partner_place = (partner_in_cycle * STRIPS + partner_strip - STRIPS // 2) % TILES
    adjacent_tile = partner_cycle * TILES + partner_place
    seam_codes = jnp.broadcast_to(face_code, (3, 4, STRIPS, 2))
    adjacent_tile = jnp.roll(adjacent_tile.reshape(3, TILES, 2), -(STRIPS // 2), axis=1)
    seam_codes = jnp.roll(seam_codes.reshape(3, TILES, 2), -(STRIPS // 2), axis=1)
    return (adjacent_tile.astype(jnp.int32), seam_codes.astype(jnp.int32))


def draw_seam_tile(key, part):
    return seam_layout(key)[0]


def draw_seam_code(key, part):
    return seam_layout(key)[1]


def level_of(rng, dims, shards, smallest, high):
    factor_of = 1.0
    for axis_at, blocks in shards:
        steps = jax.random.uniform(jax.random.fold_in(jax.random.fold_in(rng, 6), axis_at), (blocks,), jnp.float32, smallest / len(shards), high / len(shards))
        factor_of = factor_of * jnp.repeat(jnp.exp(steps), dims[axis_at] // blocks).reshape((-1,) + (1,) * (len(dims) - 1 - axis_at))
    return factor_of


def bell_draw(rng, shape, spread, limit, shards=(), kind=jnp.bfloat16):
    entries = jax.random.normal(rng, shape, jnp.float32) * spread
    if len(shards) > 0:
        entries = level_of(rng, shape, shards, -0.22, 0.18) * entries
    return jnp.clip(entries, min=-limit, max=limit).astype(kind)


def setup_inputs(seed: int = 0, part: int = 0) -> dict:
    seeds = jax.random.split(jax.random.key(seed), 12)
    part_splits = jax.random.split(jax.random.fold_in(seeds[11], part), 12)
    fields = bell_draw(part_splits[0], (3, ROWS, COLS, C), 1.0, 6.0, ((1, 16),))
    seam_tile = draw_seam_tile(jax.random.fold_in(seeds[11], 71), part)
    seam_code = draw_seam_code(jax.random.fold_in(seeds[11], 71), part)
    encoder_weight = bell_draw(seeds[3], (3, 3, C, C), (9 * C) ** -0.5, 0.125)
    encoder_bias = bell_draw(seeds[4], (C,), 0.5, 3.0, (), jnp.float32)
    middle_weight = bell_draw(seeds[5], (3, 3, C, C), (9 * C) ** -0.5, 0.125)
    middle_bias = bell_draw(seeds[6], (C,), 0.5, 3.0, (), jnp.float32)
    upconv_weight = bell_draw(seeds[7], (2, 2, C, C), C ** -0.5, 0.375)
    upconv_bias = bell_draw(seeds[8], (C,), 0.5, 3.0, (), jnp.float32)
    decoder_weight = bell_draw(seeds[9], (3, 3, 2 * C, C), (18 * C) ** -0.5, 0.09375)
    decoder_offset_bias = bell_draw(seeds[10], (C,), 0.5, 3.0, (), jnp.float32)
    return dict(fields=fields, seam_tile=seam_tile, seam_code=seam_code, encoder_weight=encoder_weight, encoder_bias=encoder_bias, middle_weight=middle_weight, middle_bias=middle_bias, upconv_weight=upconv_weight, upconv_bias=upconv_bias, decoder_weight=decoder_weight, decoder_offset_bias=decoder_offset_bias)


def gelu_tanh(values):
    return jax.nn.gelu(values, approximate=True)


def blank_edge_rows(extended, top_face, bottom_face):
    upper_row = extended[..., :1, :, :]
    lower_row = extended[..., -1:, :, :]
    upper_row = jnp.where(top_face, jnp.zeros_like(upper_row), upper_row)
    lower_row = jnp.where(bottom_face, jnp.zeros_like(lower_row), lower_row)
    return jnp.concatenate([upper_row, extended[..., 1:-1, :, :], lower_row], axis=-3)


def boundary_columns(extended):
    return jnp.stack([extended[..., :, 0, :], extended[..., :, -1, :]], axis=-3)


def pick_partner(flattened, partners, seam_codes):
    chosen = flattened[partners]
    column_bit = (seam_codes % 2)[..., None, None]
    single = jnp.where(column_bit == 0, chosen[..., 0, :, :], chosen[..., 1, :, :])
    mirror_flag = (seam_codes // 2)[..., None, None]
    return jnp.where(mirror_flag == 1, single[..., ::-1, :], single)


def attach_columns(extended, picked):
    left_col = picked[..., 0, :, :][..., :, None, :]
    right_col = picked[..., 1, :, :][..., :, None, :]
    return jnp.concatenate([left_col, extended, right_col], axis=-2)


def convolve(padded, weight, bias):
    leading = padded.shape[:-3]
    rows_out = padded.shape[-3] - 2
    cols_out = padded.shape[-2] - 2
    chans_in = padded.shape[-1]
    chans_out = weight.shape[-1]
    accumulated = jnp.zeros(leading + (rows_out, cols_out, chans_out), jnp.float32)
    for row_tap in range(3):
        for col_tap in range(3):
            window = padded[..., row_tap:row_tap + rows_out, col_tap:col_tap + cols_out, :]
            product = jnp.dot(window.reshape(-1, chans_in), weight[row_tap, col_tap], preferred_element_type=jnp.float32)
            accumulated = accumulated + product.reshape(accumulated.shape)
    return accumulated + bias


def coarsen_grid(sphere_map):
    leading = sphere_map.shape[:-3]
    rows_in, cols_in, chans_in = sphere_map.shape[-3:]
    values = sphere_map.astype(jnp.float32).reshape(leading + (rows_in // 2, 2, cols_in // 2, 2, chans_in))
    return jnp.mean(values, axis=(-4, -2)).astype(jnp.bfloat16)


def upsample(coarse, weight, bias):
    leading = coarse.shape[:-3]
    rows_in, cols_in, chans_in = coarse.shape[-3:]
    chans_out = weight.shape[-1]
    flattened = coarse.reshape(-1, chans_in)
    phases = []
    for row_phase in range(2):
        phase_row = []
        for col_phase in range(2):
            product = jnp.dot(flattened, weight[row_phase, col_phase], preferred_element_type=jnp.float32)
            phase_row.append(product.reshape(leading + (rows_in, cols_in, chans_out)))
        phases.append(jnp.stack(phase_row, axis=-2).reshape(leading + (rows_in, 2 * cols_in, chans_out)))
    full = jnp.stack(phases, axis=-3).reshape(leading + (2 * rows_in, 2 * cols_in, chans_out))
    return (full + bias).astype(jnp.bfloat16)


def pad_field(sphere_map, partners, seam_codes):
    rows_in = sphere_map.shape[1] // TILES
    tiles = sphere_map.reshape(3, TILES, rows_in, sphere_map.shape[2], sphere_map.shape[3])
    upper_row = jnp.roll(tiles[:, :, -1:], 1, axis=1)
    lower_row = jnp.roll(tiles[:, :, :1], -1, axis=1)
    extended = jnp.concatenate([upper_row, tiles, lower_row], axis=2)
    strip_index = ((jnp.arange(TILES, dtype=jnp.int32) + STRIPS // 2) % STRIPS).reshape(1, TILES, 1, 1, 1)
    extended = blank_edge_rows(extended, strip_index == 0, strip_index == STRIPS - 1)
    edges = boundary_columns(extended)
    flattened = edges.reshape((3 * TILES,) + edges.shape[2:])
    return attach_columns(extended, pick_partner(flattened, partners, seam_codes))


def reference(fields, seam_tile, seam_code, encoder_weight, encoder_bias, middle_weight, middle_bias, upconv_weight, upconv_bias, decoder_weight, decoder_offset_bias):
    padded = pad_field(fields, seam_tile, seam_code)
    shortcut_map = gelu_tanh(convolve(padded, encoder_weight, encoder_bias)).astype(jnp.bfloat16)
    shortcut_map = shortcut_map.reshape(3, ROWS, COLS, C)
    averaged_map = coarsen_grid(shortcut_map)
    padded = pad_field(averaged_map, seam_tile, seam_code)
    coarse = gelu_tanh(convolve(padded, middle_weight, middle_bias)).astype(jnp.bfloat16)
    coarse = coarse.reshape(3, ROWS // 2, COLS // 2, C)
    upsampled = upsample(coarse, upconv_weight, upconv_bias)
    joined = jnp.concatenate([upsampled, shortcut_map], axis=-1)
    padded = pad_field(joined, seam_tile, seam_code)
    decoded = convolve(padded, decoder_weight, decoder_offset_bias).astype(jnp.bfloat16)
    return decoded.reshape(3, ROWS, COLS, C)
```

```python
import functools

import jax
import jax.numpy as jnp
from jax import lax
from jax.experimental import pallas as pl
from jax.experimental.pallas import tpu as pltpu
from jax.sharding import PartitionSpec as P

F32 = jnp.float32
BF16 = jnp.bfloat16
FACES = 4
SUB = 16


def gelu_tanh(x):
    return 0.5 * x * (1.0 + jnp.tanh(0.7978845608 * (x + 0.044715 * (x * x * x))))


def kernel(
    tiles,
    seam_tile,
    seam_code,
    fields_hbm,
    enc_w_hbm,
    mid_w_hbm,
    up_w_hbm,
    dec_w_hbm,
    enc_b,
    mid_b,
    up_b,
    dec_b,
    out,
    fields,
    enc_w,
    mid_w,
    up_w,
    dec_w,
    x_enc,
    x_skip,
    x_pool,
    x_up,
    coarse,
    acc_dec,
    pre,
    pixels,
    terms,
    p_in,
    p_out,
    edge_tmp,
    corner_tmp,
    seam_tmp,
    corner_src,
    edges_enc,
    edges_pool,
    edges_skip,
    edges_coarse,
    recv_enc,
    recv_pool,
    recv_skip,
    recv_coarse,
    corner_enc,
    corner_pool,
    corner_skip,
    corner_coarse,
    load_sem,
    send_sem,
    recv_sem,
):
    recv_corners = (corner_enc, corner_pool, corner_skip, corner_coarse)
    cycles, h, cols, ch = fields.shape
    hc = h // 2
    planes = cols // SUB
    cplanes = planes // 2
    strips = tiles // FACES
    me = lax.axis_index("tile")
    place = lax.rem(me + strips // 2, tiles)
    face = place // strips
    strip = place - face * strips
    top_face = strip == 0
    bottom_face = strip == strips - 1
    has_above = strip > 0
    has_below = strip < strips - 1
    up_tile = lax.rem(me + tiles - 1, tiles)
    down_tile = lax.rem(me + 1, tiles)
    at_sub = lax.broadcasted_iota(jnp.int32, (SUB, ch), 0)

    def tile_of(f, s):
        return lax.rem(f * strips + s + tiles - strips // 2, tiles)

    faces = [lax.rem(face + j, FACES) for j in range(FACES)]

    loads = []
    for k, (src, dst) in enumerate(
        ((fields_hbm, fields), (enc_w_hbm, enc_w), (dec_w_hbm, dec_w), (mid_w_hbm, mid_w), (up_w_hbm, up_w))
    ):
        copy = pltpu.make_async_copy(src, dst, load_sem.at[k])
        copy.start()
        loads.append(copy)

    barrier = pltpu.get_barrier_semaphore()

    @pl.loop(1, tiles)
    def _(k):
        pl.semaphore_signal(barrier, inc=1, device_id={"tile": lax.rem(me + k, tiles)})

    def remote(src, dst, e, send_at, recv_at, target):
        return pltpu.make_async_remote_copy(
            src_ref=src,
            dst_ref=dst,
            send_sem=send_sem.at[e, send_at],
            recv_sem=recv_sem.at[e, recv_at],
            device_id={"tile": target},
        )

    def shifted(value, last):
        if last:
            return jnp.where(at_sub == SUB - 1, 0.0, pltpu.roll(value, SUB - 1, 0)).astype(BF16)
        return jnp.where(at_sub == 0, 0.0, pltpu.roll(value, 1, 0)).astype(BF16)

    class Exchange:
        def __init__(self, e, rows, edge_ref, recv_ref, top, bottom, above, below):
            self.e, self.rows, self.edges, self.recv = e, rows, edge_ref, recv_ref
            self.top, self.bottom, self.above, self.below = top, bottom, above, below

        def publish(self):
            e, rows = self.e, self.rows
            value = edge_tmp[e, :, 0:rows, :].astype(BF16)
            self.edges[...] = value
            self.recv[face] = value
            for k in range(2 * cycles):
                corner_tmp[e, 0, k : k + 1, :] = edge_tmp[e, k, 0:1, :]
                corner_tmp[e, 1, k : k + 1, :] = edge_tmp[e, k, rows - 1 : rows, :]
            for which in range(2):
                corner_src[e, which] = corner_tmp[e, which].astype(BF16)

            @pl.when(strip == strips // 2 - 1)
            def _():
                recv_corners[e][1, FACES + face] = corner_tmp[e, 1].astype(BF16)

            @pl.when(strip == strips // 2)
            def _():
                recv_corners[e][0, FACES + face] = corner_tmp[e, 0].astype(BF16)

        def seam_copies(self):
            copies = []
            for kind in range(2):
                s = strip if kind == 0 else strips - 1 - strip
                for f in faces[1 - kind :]:
                    at = 2 + kind * FACES
                    copies.append(
                        remote(
                            self.edges,
                            self.recv.at[kind * FACES + face],
                            self.e,
                            at + f,
                            at + face,
                            tile_of(f, s),
                        )
                    )
            return copies

        def corner_copies(self):
            groups = []
            for which, s, pos, kind, cond, own in (
                (1, strip + 1, 0, 0, has_below, None),
                (1, strips - 2 - strip, 1, 1, has_below, strip != strips // 2 - 1),
                (0, strip + strips - 1, 1, 0, has_above, None),
                (0, strips - strip, 0, 1, has_above, strip != strips // 2),
            ):
                slot = kind * FACES + face
                at = 10 + 8 * pos
                for j, f in enumerate(faces):
                    copy = remote(
                        corner_src.at[self.e, which],
                        recv_corners[self.e].at[pos, slot],
                        self.e,
                        at + kind * FACES + f,
                        at + slot,
                        lax.rem(tile_of(f, s) + (tiles - strips if which == 0 and kind == 0 else 0), tiles),
                    )
                    ok = cond
                    if j == 0 and own is not None:
                        ok = jnp.logical_and(cond, own)
                    groups.append((ok, copy))
            return groups

        def row_copies(self):
            return [
                (has_below, remote(self.bottom, self.above, self.e, 0, 0, down_tile)),
                (has_above, remote(self.top, self.below, self.e, 1, 1, up_tile)),
            ]

        def send_seams(self):
            for copy in self.seam_copies():
                copy.start()
            for cond, copy in self.corner_copies():
                pl.when(cond)(copy.start)

        def send_rows(self):
            for cond, copy in self.row_copies():
                pl.when(cond)(copy.start)

        def wait_sends(self):
            for copy in self.seam_copies():
                copy.wait_send()
            for cond, copy in self.row_copies() + self.corner_copies():
                pl.when(cond)(copy.wait_send)

        def wait_above(self):
            remote(self.bottom, self.above, self.e, 0, 0, down_tile).wait_recv()

        def wait_below(self):
            remote(self.top, self.below, self.e, 1, 1, up_tile).wait_recv()

        def wait_seams(self):
            e = self.e
            for kind in range(2):
                for f in faces[1 - kind :]:
                    slot = kind * FACES + f
                    remote(self.edges, self.recv.at[slot], e, 2 + slot, 2 + slot, up_tile).wait_recv()
            for pos, cond, mid in ((0, has_above, strips // 2), (1, has_below, strips // 2 - 1)):
                for kind in range(2):
                    for j, f in enumerate(faces):
                        slot = kind * FACES + f
                        at = 10 + 8 * pos + slot
                        ok = cond
                        if j == 0 and kind == 1:
                            ok = jnp.logical_and(cond, strip != mid)
                        copy = remote(corner_src.at[e, 0], recv_corners[e].at[pos, slot], e, at, at, up_tile)
                        pl.when(ok)(copy.wait_recv)

        def load_seams(self):
            rows, e = self.rows, self.e
            at = lax.broadcasted_iota(jnp.int32, (8, ch), 0)
            for side in range(2):
                for r in range(cycles):
                    partner, code = seam_tile[side, r], seam_code[side, r]
                    cycle = partner // tiles
                    home = lax.rem(partner - cycle * tiles + strips // 2, tiles) // strips
                    mirrored = code >= 2
                    slot = jnp.where(mirrored, FACES, 0) + home
                    k = 2 * cycle + lax.rem(code, 2)
                    column = self.recv[slot, k].astype(F32)
                    ends = [recv_corners[e][pos, slot].astype(F32) for pos in range(2)]
                    above, below = [jnp.sum(jnp.where(at == k, end, 0.0), axis=0, keepdims=True) for end in ends]
                    seam_tmp[e, side, r, 0:1, :] = jnp.where(top_face, 0.0, above)
                    seam_tmp[e, side, r, rows + 1 : rows + 2, :] = jnp.where(bottom_face, 0.0, below)
                    for i in range(rows):
                        seam_tmp[e, side, r, i + 1 : i + 2, :] = jnp.where(
                            mirrored, column[rows - 1 - i : rows - i], column[i : i + 1]
                        )

    def seam_term(e, side, weight):
        lhs = [
            jnp.concatenate([seam_tmp[e, side, r, a : a + 8, :] for r in range(cycles)], axis=0) for a in range(3)
        ]
        return jnp.dot(jnp.concatenate(lhs, axis=1).astype(BF16), weight, preferred_element_type=F32)

    def conv(x, i, n, q, weight):
        taps = [
            x[pl.ds(i + a, n), b : b + q].reshape(n * q * cycles * SUB, ch) for a in range(3) for b in range(3)
        ]
        product = jnp.dot(jnp.concatenate(taps, axis=1), weight, preferred_element_type=F32)
        return product.reshape(n, q, cycles, SUB, ch)

    def keep_ends(stage, i, value):
        for r in range(cycles):
            pre[stage, 0, pl.ds(8 * r + i, 1), :] = value[0, r, 0:1, :]
            pre[stage, 1, pl.ds(8 * r + i, 1), :] = value[-1, r, SUB - 1 : SUB, :]

    def put_row(x, i, value):
        q = value.shape[0]
        x[i, 1 : q + 1] = value.astype(BF16)
        for r in range(cycles):
            x[i, 0, r] = shifted(value[q - 1, r], False)
            x[i, q + 1, r] = shifted(value[0, r], True)

    def halo_row(x, i, q, wait, missing):
        @pl.when(missing)
        def _():
            x[i] = jnp.zeros(x.shape[1:], BF16)

        @pl.when(jnp.logical_not(missing))
        def _():
            wait()
            for r in range(cycles):
                x[i, 0, r] = shifted(x[i, q, r].astype(F32), False)
                x[i, q + 1, r] = shifted(x[i, 1, r].astype(F32), True)

    def fix_ends(stage, ex, rows, term_of, tile_ref):
        for side in range(2):
            value = gelu_tanh(pre[stage, side] + term_of(side))
            pixels[side] = value
            for r in range(cycles):
                edge_tmp[ex.e, 2 * r + side, 0:rows, :] = value[8 * r : 8 * r + rows]
        for side in range(2):
            for r in range(cycles):
                for i in range(rows):
                    tile = tile_ref(i, side, r)
                    row = pixels[side, 8 * r + i : 8 * r + i + 1, :]
                    tile[...] = jnp.where(at_sub == side * (SUB - 1), row, tile[...].astype(F32)).astype(BF16)

    def steps(lo, hi, most, body):
        count = hi - lo
        unroll = max(u for u in range(1, most + 1) if count % u == 0)

        @pl.loop(0, count // unroll)
        def _(k):
            for u in range(unroll):
                body(lo + k * unroll + u)

    wide = (planes + 2) * SUB
    m = lax.broadcasted_iota(jnp.int32, (wide, cols), 0)
    j = lax.broadcasted_iota(jnp.int32, (wide, cols), 1)
    plane = m // SUB
    p_in[...] = jnp.where((m - plane * SUB) * planes + plane - 1 == j, 1.0, 0.0).astype(BF16)
    m = lax.broadcasted_iota(jnp.int32, (cols, cols), 0)
    j = lax.broadcasted_iota(jnp.int32, (cols, cols), 1)
    plane = j // SUB
    p_out[...] = jnp.where((j - plane * SUB) * planes + plane == m, 1.0, 0.0).astype(BF16)

    enc = Exchange(
        0, h, edges_enc, recv_enc, *[x_enc.at[i, 1 : planes + 1] for i in (1, h, 0, h + 1)]
    )
    pool = Exchange(
        1, hc, edges_pool, recv_pool, *[x_pool.at[i, 1 : cplanes + 1] for i in (1, hc, 0, hc + 1)]
    )
    skip = Exchange(
        2, h, edges_skip, recv_skip, *[x_skip.at[i, 1 : planes + 1] for i in (1, h, 0, h + 1)]
    )
    low = Exchange(3, hc, edges_coarse, recv_coarse, *[coarse.at[i] for i in (1, hc, 0, hc + 1)])

    loads[0].wait()
    for r in range(cycles):
        for i in range(h):
            edge_tmp[0, 2 * r, i : i + 1, :] = fields[r, i, 0:SUB, :].astype(F32)[0:1]
            edge_tmp[0, 2 * r + 1, i : i + 1, :] = fields[r, i, cols - SUB : cols, :].astype(F32)[SUB - 1 : SUB]
    enc.publish()

    def to_planes(i):
        for r in range(cycles):
            row = jnp.dot(p_in[...], fields[r, i], preferred_element_type=F32)
            x_enc[i + 1, :, r] = row.astype(BF16).reshape(planes + 2, SUB, ch)

    steps(0, h, 2, to_planes)
    pl.semaphore_wait(barrier, tiles - 1)
    enc.send_seams()
    enc.send_rows()

    loads[1].wait()

    def enc_row(i):
        value = conv(x_enc, i, 1, planes, enc_w[...].reshape(9 * ch, ch))[0] + enc_b[...]
        keep_ends(0, i, value)
        put_row(x_skip, i + 1, gelu_tanh(value))

    steps(1, h - 1, 3, enc_row)
    halo_row(x_enc, 0, planes, enc.wait_above, top_face)
    halo_row(x_enc, h + 1, planes, enc.wait_below, bottom_face)
    enc_row(0)
    enc_row(h - 1)
    enc.wait_seams()
    enc.load_seams()
    fix_ends(
        0,
        skip,
        h,
        lambda side: seam_term(0, side, enc_w[:, 2 * side].reshape(3 * ch, ch)),
        lambda i, side, r: x_skip.at[i + 1, planes if side else 1, r],
    )

    for q in range(hc):
        parts = []
        for k in range(cplanes):
            total = None
            for a in range(2):
                for b in range(2):
                    term = x_skip[2 * q + a + 1, 2 * k + b + 1].astype(F32)
                    total = term if total is None else total + term
            parts.append((total * 0.25)[None])
        value = jnp.concatenate(parts, axis=0)
        put_row(x_pool, q + 1, value)
        for r in range(cycles):
            edge_tmp[1, 2 * r, q : q + 1, :] = value[0, r, 0:1, :]
            edge_tmp[1, 2 * r + 1, q : q + 1, :] = value[-1, r, SUB - 1 : SUB, :]
    pool.publish()
    pool.send_seams()
    pool.send_rows()
    skip.publish()
    skip.send_seams()
    skip.send_rows()

    loads[2].wait()

    def dec_weights(part):
        picked = [dec_w[a, b, part * ch : (part + 1) * ch, :] for a in range(3) for b in range(3)]
        return jnp.concatenate(picked, axis=0)

    def dec_side(part, side):
        picked = [dec_w[a, 2 * side, part * ch : (part + 1) * ch, :] for a in range(3)]
        return jnp.concatenate(picked, axis=0)

    def dec_skip_row(i):
        acc_dec[i] = conv(x_skip, i, 1, planes, dec_weights(1))[0]

    steps(1, h - 1, 3, dec_skip_row)

    loads[3].wait()
    loads[4].wait()

    def mid_rows(i, n):
        value = conv(x_pool, i, n, cplanes, mid_w[...].reshape(9 * ch, ch)) + mid_b[...]
        for u in range(n):
            keep_ends(1, i + u, value[u])
        coarse[pl.ds(i + 1, n)] = gelu_tanh(value).astype(BF16)

    mid_rows(1, hc - 2)
    halo_row(x_pool, 0, cplanes, pool.wait_above, top_face)
    halo_row(x_pool, hc + 1, cplanes, pool.wait_below, bottom_face)
    mid_rows(0, 1)
    mid_rows(hc - 1, 1)
    pool.wait_seams()
    pool.load_seams()
    fix_ends(
        1,
        low,
        hc,
        lambda side: seam_term(1, side, mid_w[:, 2 * side].reshape(3 * ch, ch)),
        lambda i, side, r: coarse.at[i + 1, cplanes - 1 if side else 0, r],
    )
    low.publish()
    low.send_seams()
    low.send_rows()

    def up_rows(q, first, last):
        lhs = coarse[q].reshape(cplanes * cycles * SUB, ch)
        weight = jnp.concatenate([up_w[a, b] for a in range(first, last) for b in range(2)], axis=1)
        product = jnp.dot(lhs, weight, preferred_element_type=F32)
        for a in range(first, last):
            row = [None] * planes
            for b in range(2):
                at = (2 * (a - first) + b) * ch
                value = (product[:, at : at + ch] + up_b[...]).reshape(cplanes, cycles, SUB, ch)
                for k in range(cplanes):
                    row[2 * k + b] = value[k : k + 1]
            put_row(x_up, 2 * q + a - 1, jnp.concatenate(row, axis=0))

    for q in range(hc):
        up_rows(q + 1, 0, 2)

    def dec_up_row(i):
        value = acc_dec[i] + conv(x_up, i, 1, planes, dec_weights(0))[0] + dec_b[...]
        keep_ends(2, i, value)
        value = value.astype(BF16)
        for r in range(cycles):
            row = jnp.dot(p_out[...], value[:, r].reshape(cols, ch), preferred_element_type=F32)
            out[r, i] = row.astype(BF16)

    steps(1, h - 1, 3, dec_up_row)
    halo_row(x_skip, 0, planes, skip.wait_above, top_face)
    halo_row(x_skip, h + 1, planes, skip.wait_below, bottom_face)
    dec_skip_row(0)
    dec_skip_row(h - 1)
    skip.wait_seams()
    skip.load_seams()
    for side in range(2):
        terms[side] = seam_term(2, side, dec_side(1, side))

    for row, q, a, missing, wait in (
        (0, 0, 1, top_face, low.wait_above),
        (h + 1, hc + 1, 0, bottom_face, low.wait_below),
    ):

        @pl.when(missing)
        def _():
            x_up[row] = jnp.zeros(x_up.shape[1:], BF16)

        @pl.when(jnp.logical_not(missing))
        def _():
            wait()
            up_rows(q, a, a + 1)

    dec_up_row(0)
    dec_up_row(h - 1)

    low.wait_seams()
    low.load_seams()
    lhs = jnp.concatenate([seam_tmp[3, side, r, 0:8, :] for side in range(2) for r in range(cycles)], axis=0)
    weight = jnp.concatenate([up_w[a, b] for a in range(2) for b in range(2)], axis=1)
    product = jnp.dot(lhs.astype(BF16), weight, preferred_element_type=F32)
    for side in range(2):
        for r in range(cycles):
            code = seam_code[side, r]
            last = lax.rem(code, 2) == 1
            mirrored = code >= 2
            at = 8 * (side * cycles + r)
            phases = []
            for a in range(2):
                pair = [product[at : at + 8, (2 * a + b) * ch : (2 * a + b + 1) * ch] for b in range(2)]
                phases.append(jnp.where(last, pair[1], pair[0]) + up_b[...])
            even = jnp.where(mirrored, phases[1], phases[0])
            odd = jnp.where(mirrored, phases[0], phases[1])
            seam_tmp[4, side, r, 0:1, :] = jnp.where(top_face, 0.0, odd[0:1])
            for k in range(hc):
                seam_tmp[4, side, r, 2 * k + 1 : 2 * k + 2, :] = even[k + 1 : k + 2]
                seam_tmp[4, side, r, 2 * k + 2 : 2 * k + 3, :] = odd[k + 1 : k + 2]
            seam_tmp[4, side, r, h + 1 : h + 2, :] = jnp.where(bottom_face, 0.0, even[hc + 1 : hc + 2])
    for side in range(2):
        pixels[side] = pre[2, side] + terms[side] + seam_term(4, side, dec_side(0, side))
    for side in range(2):
        lo = side * (cols - SUB)
        for r in range(cycles):
            for i in range(h):
                row = pixels[side, 8 * r + i : 8 * r + i + 1, :]
                tile = out[r, i, lo : lo + SUB, :].astype(F32)
                out[r, i, lo : lo + SUB, :] = jnp.where(at_sub == side * (SUB - 1), row, tile).astype(BF16)

    for ex in (enc, pool, skip, low):
        ex.wait_sends()


def solution(mesh):
    tiles = mesh.shape["tile"]

    def on_device(fields, seam_tile, seam_code, enc_w, enc_b, mid_w, mid_b, up_w, up_b, dec_w, dec_b):
        cycles, h, cols, ch = fields.shape
        hc = h // 2
        planes = cols // SUB
        cplanes = planes // 2
        vmem = pl.BlockSpec(memory_space=pltpu.VMEM)
        smem = pl.BlockSpec(memory_space=pltpu.SMEM)
        hbm = pl.BlockSpec(memory_space=pl.ANY)
        ends = 2 * cycles
        slots = 2 * FACES
        return pl.pallas_call(
            functools.partial(kernel, tiles),
            out_shape=jax.ShapeDtypeStruct(fields.shape, BF16),
            in_specs=[smem, smem] + [hbm] * 5 + [vmem] * 4,
            out_specs=vmem,
            scratch_shapes=[
                pltpu.VMEM(fields.shape, BF16),
                pltpu.VMEM(enc_w.shape, BF16),
                pltpu.VMEM(mid_w.shape, BF16),
                pltpu.VMEM(up_w.shape, BF16),
                pltpu.VMEM(dec_w.shape, BF16),
                pltpu.VMEM((h + 2, planes + 2, cycles, SUB, ch), BF16),
                pltpu.VMEM((h + 2, planes + 2, cycles, SUB, ch), BF16),
                pltpu.VMEM((hc + 2, cplanes + 2, cycles, SUB, ch), BF16),
                pltpu.VMEM((h + 2, planes + 2, cycles, SUB, ch), BF16),
                pltpu.VMEM((hc + 2, cplanes, cycles, SUB, ch), BF16),
                pltpu.VMEM((h, planes, cycles, SUB, ch), F32),
                pltpu.VMEM((3, 2, 8 * cycles, ch), F32),
                pltpu.VMEM((2, 8 * cycles, ch), F32),
                pltpu.VMEM((2, 8 * cycles, ch), F32),
                pltpu.VMEM(((planes + 2) * SUB, cols), BF16),
                pltpu.VMEM((cols, cols), BF16),
                pltpu.VMEM((4, ends, 8, ch), F32),
                pltpu.VMEM((4, 2, 8, ch), F32),
                pltpu.VMEM((5, 2, cycles, 16, ch), F32),
                pltpu.VMEM((4, 2, 8, ch), BF16),
                pltpu.VMEM((ends, h, ch), BF16),
                pltpu.VMEM((ends, hc, ch), BF16),
                pltpu.VMEM((ends, h, ch), BF16),
                pltpu.VMEM((ends, hc, ch), BF16),
                pltpu.VMEM((slots, ends, h, ch), BF16),
                pltpu.VMEM((slots, ends, hc, ch), BF16),
                pltpu.VMEM((slots, ends, h, ch), BF16),
                pltpu.VMEM((slots, ends, hc, ch), BF16),
                pltpu.VMEM((2, slots, 8, ch), BF16),
                pltpu.VMEM((2, slots, 8, ch), BF16),
                pltpu.VMEM((2, slots, 8, ch), BF16),
                pltpu.VMEM((2, slots, 8, ch), BF16),
                pltpu.SemaphoreType.DMA((5,)),
                pltpu.SemaphoreType.DMA((4, 10 + 2 * slots)),
                pltpu.SemaphoreType.DMA((4, 10 + 2 * slots)),
            ],
            compiler_params=pltpu.CompilerParams(
                collective_id=0, has_side_effects=True, vmem_limit_bytes=60 * 1024 * 1024
            ),
        )(
            jnp.transpose(seam_tile, (1, 2, 0)).reshape(2, cycles),
            jnp.transpose(seam_code, (1, 2, 0)).reshape(2, cycles),
            fields,
            enc_w,
            mid_w,
            up_w,
            dec_w,
            enc_b.reshape(1, ch),
            mid_b.reshape(1, ch),
            up_b.reshape(1, ch),
            dec_b.reshape(1, ch),
        )

    return jax.shard_map(
        on_device,
        mesh=mesh,
        in_specs=(P("grp", "tile", None, None), P(None, "tile", None), P(None, "tile", None)) + (P(),) * 8,
        out_specs=P("grp", "tile", None, None),
        check_vma=False,
    )
```

```python
import functools

import jax
import jax.numpy as jnp
from jax import lax
from jax.experimental import pallas as pl
from jax.experimental.pallas import tpu as pltpu
from jax.sharding import PartitionSpec as P

F32 = jnp.float32
BF16 = jnp.bfloat16
FACES = 4
SUB = 16


def gelu_tanh(x):
    return 0.5 * x * (1.0 + jnp.tanh(0.7978845608 * (x + 0.044715 * (x * x * x))))


def kernel(
    tiles,
    seam_tile,
    seam_code,
    fields_hbm,
    enc_w_hbm,
    mid_w_hbm,
    up_w_hbm,
    dec_w_hbm,
    enc_b,
    mid_b,
    up_b,
    dec_b,
    out,
    fields,
    enc_w,
    mid_w,
    up_w,
    dec_w,
    x_enc,
    x_skip,
    x_pool,
    x_up,
    coarse,
    acc_dec,
    pre,
    pixels,
    terms,
    p_in,
    p_out,
    edge_tmp,
    corner_tmp,
    seam_tmp,
    corner_src,
    edges_enc,
    edges_pool,
    edges_skip,
    edges_coarse,
    recv_enc,
    recv_pool,
    recv_skip,
    recv_coarse,
    corner_enc,
    corner_pool,
    corner_skip,
    corner_coarse,
    load_sem,
    send_sem,
    recv_sem,
):
    recv_corners = (corner_enc, corner_pool, corner_skip, corner_coarse)
    cycles, h, cols, ch = fields.shape
    hc = h // 2
    planes = cols // SUB
    cplanes = planes // 2
    strips = tiles // FACES
    me = lax.axis_index("tile")
    place = lax.rem(me + strips // 2, tiles)
    face = place // strips
    strip = place - face * strips
    top_face = strip == 0
    bottom_face = strip == strips - 1
    has_above = strip > 0
    has_below = strip < strips - 1
    send_top = jnp.logical_and(has_above, strip != strips // 2)
    send_bottom = jnp.logical_and(has_below, strip != strips // 2 - 1)
    up_tile = lax.rem(me + tiles - 1, tiles)
    down_tile = lax.rem(me + 1, tiles)
    at_sub = lax.broadcasted_iota(jnp.int32, (SUB, ch), 0)

    def tile_of(f, s):
        return lax.rem(f * strips + s + tiles - strips // 2, tiles)

    faces = [lax.rem(face + j, FACES) for j in range(FACES)]

    loads = []
    for k, (src, dst) in enumerate(
        ((fields_hbm, fields), (enc_w_hbm, enc_w), (dec_w_hbm, dec_w), (mid_w_hbm, mid_w), (up_w_hbm, up_w))
    ):
        copy = pltpu.make_async_copy(src, dst, load_sem.at[k])
        copy.start()
        loads.append(copy)

    barrier = pltpu.get_barrier_semaphore()

    @pl.loop(1, tiles)
    def _(k):
        pl.semaphore_signal(barrier, inc=1, device_id={"tile": lax.rem(me + k, tiles)})

    def remote(src, dst, e, send_at, recv_at, target):
        return pltpu.make_async_remote_copy(
            src_ref=src,
            dst_ref=dst,
            send_sem=send_sem.at[e, send_at],
            recv_sem=recv_sem.at[e, recv_at],
            device_id={"tile": target},
        )

    def shifted(value, last):
        if last:
            return jnp.where(at_sub == SUB - 1, 0.0, pltpu.roll(value, SUB - 1, 0)).astype(BF16)
        return jnp.where(at_sub == 0, 0.0, pltpu.roll(value, 1, 0)).astype(BF16)

    class Exchange:
        def __init__(self, e, rows, edge_ref, recv_ref, top, bottom, above, below):
            self.e, self.rows, self.edges, self.recv = e, rows, edge_ref, recv_ref
            self.top, self.bottom, self.above, self.below = top, bottom, above, below

        def publish(self):
            e, rows = self.e, self.rows
            value = edge_tmp[e, :, 0:rows, :].astype(BF16)
            self.edges[...] = value
            self.recv[face] = value
            for k in range(2 * cycles):
                corner_tmp[e, 0, k : k + 1, :] = edge_tmp[e, k, 0:1, :]
                corner_tmp[e, 1, k : k + 1, :] = edge_tmp[e, k, rows - 1 : rows, :]
            for which in range(2):
                corner_src[e, which] = corner_tmp[e, which].astype(BF16)

        def send_seams(self):
            e = self.e
            for kind in range(2):
                s = strip if kind == 0 else strips - 1 - strip
                for f in faces[1 - kind :]:
                    remote(self.edges, self.recv.at[kind * FACES + face], e, 2, 2, tile_of(f, s)).start()

            def corner(which, pos, kind, s):
                for f in faces:
                    dst = recv_corners[e].at[pos, kind * FACES + face]
                    remote(corner_src.at[e, which], dst, e, 3 + which, 3 + pos, tile_of(f, s)).start()

            @pl.when(send_bottom)
            def _():
                corner(1, 0, 0, strip + 1)
                corner(1, 1, 1, strips - 2 - strip)

            @pl.when(send_top)
            def _():
                corner(0, 1, 0, strip - 1)
                corner(0, 0, 1, strips - strip)

        def row_copies(self):
            return [
                (has_below, remote(self.bottom, self.above, self.e, 0, 0, down_tile)),
                (has_above, remote(self.top, self.below, self.e, 1, 1, up_tile)),
            ]

        def send_rows(self):
            for cond, copy in self.row_copies():
                pl.when(cond)(copy.start)

        def seam_wait(self):
            others = self.recv.at[pl.ds(0, 2 * FACES - 1)]
            return remote(others, others, self.e, 2, 2, up_tile)

        def corner_wait(self, at):
            whole = recv_corners[self.e].at[at]
            return remote(whole, whole, self.e, 3 + at, 3 + at, up_tile)

        def wait_sends(self):
            self.seam_wait().wait_send()
            pl.when(send_top)(self.corner_wait(0).wait_send)
            pl.when(send_bottom)(self.corner_wait(1).wait_send)
            for cond, copy in self.row_copies():
                pl.when(cond)(copy.wait_send)

        def wait_above(self):
            remote(self.bottom, self.above, self.e, 0, 0, down_tile).wait_recv()

        def wait_below(self):
            remote(self.top, self.below, self.e, 1, 1, up_tile).wait_recv()

        def wait_seams(self):
            self.seam_wait().wait_recv()
            pl.when(jnp.logical_and(has_above, strip != strips // 2))(self.corner_wait(0).wait_recv)
            pl.when(jnp.logical_and(has_below, strip != strips // 2 - 1))(self.corner_wait(1).wait_recv)

        def load_seams(self):
            rows, e = self.rows, self.e
            at = lax.broadcasted_iota(jnp.int32, (8, ch), 0)
            for side in range(2):
                for r in range(cycles):
                    partner, code = seam_tile[side, r], seam_code[side, r]
                    cycle = partner // tiles
                    home = lax.rem(partner - cycle * tiles + strips // 2, tiles) // strips
                    mirrored = code >= 2
                    slot = jnp.where(mirrored, FACES, 0) + home
                    k = 2 * cycle + lax.rem(code, 2)
                    column = self.recv[slot, k].astype(F32)
                    twin = self.recv[jnp.where(mirrored, 0, FACES) + home, k].astype(F32)
                    first, last = twin[0:1], twin[rows - 1 : rows]
                    ends = [recv_corners[e][pos, slot].astype(F32) for pos in range(2)]
                    above, below = [jnp.sum(jnp.where(at == k, end, 0.0), axis=0, keepdims=True) for end in ends]
                    above = jnp.where(strip == strips // 2, jnp.where(mirrored, first, last), above)
                    below = jnp.where(strip == strips // 2 - 1, jnp.where(mirrored, last, first), below)
                    seam_tmp[e, side, r, 0:1, :] = jnp.where(top_face, 0.0, above)
                    seam_tmp[e, side, r, rows + 1 : rows + 2, :] = jnp.where(bottom_face, 0.0, below)
                    for i in range(rows):
                        seam_tmp[e, side, r, i + 1 : i + 2, :] = jnp.where(
                            mirrored, column[rows - 1 - i : rows - i], column[i : i + 1]
                        )

    def seam_term(e, side, weight):
        lhs = [
            jnp.concatenate([seam_tmp[e, side, r, a : a + 8, :] for r in range(cycles)], axis=0) for a in range(3)
        ]
        return jnp.dot(jnp.concatenate(lhs, axis=1).astype(BF16), weight, preferred_element_type=F32)

    def conv(x, i, n, q, weight):
        taps = [
            x[pl.ds(i + a, n), b : b + q].reshape(n * q * cycles * SUB, ch) for a in range(3) for b in range(3)
        ]
        product = jnp.dot(jnp.concatenate(taps, axis=1), weight, preferred_element_type=F32)
        return product.reshape(n, q, cycles, SUB, ch)

    def keep_ends(stage, i, value):
        for r in range(cycles):
            pre[stage, 0, pl.ds(8 * r + i, 1), :] = value[0, r, 0:1, :]
            pre[stage, 1, pl.ds(8 * r + i, 1), :] = value[-1, r, SUB - 1 : SUB, :]

    def put_row(x, i, value):
        q = value.shape[0]
        x[i, 1 : q + 1] = value.astype(BF16)
        for r in range(cycles):
            x[i, 0, r] = shifted(value[q - 1, r], False)
            x[i, q + 1, r] = shifted(value[0, r], True)

    def halo_row(x, i, q, wait, missing):
        @pl.when(missing)
        def _():
            x[i] = jnp.zeros(x.shape[1:], BF16)

        @pl.when(jnp.logical_not(missing))
        def _():
            wait()
            for r in range(cycles):
                x[i, 0, r] = shifted(x[i, q, r].astype(F32), False)
                x[i, q + 1, r] = shifted(x[i, 1, r].astype(F32), True)

    def fix_ends(stage, ex, rows, term_of, tile_ref):
        for side in range(2):
            value = gelu_tanh(pre[stage, side] + term_of(side))
            pixels[side] = value
            for r in range(cycles):
                edge_tmp[ex.e, 2 * r + side, 0:rows, :] = value[8 * r : 8 * r + rows]
        for side in range(2):
            for r in range(cycles):
                for i in range(rows):
                    tile = tile_ref(i, side, r)
                    row = pixels[side, 8 * r + i : 8 * r + i + 1, :]
                    tile[...] = jnp.where(at_sub == side * (SUB - 1), row, tile[...].astype(F32)).astype(BF16)

    def steps(lo, hi, most, body):
        count = hi - lo
        unroll = max(u for u in range(1, most + 1) if count % u == 0)

        @pl.loop(0, count // unroll)
        def _(k):
            for u in range(unroll):
                body(lo + k * unroll + u)

    wide = (planes + 2) * SUB
    m = lax.broadcasted_iota(jnp.int32, (wide, cols), 0)
    j = lax.broadcasted_iota(jnp.int32, (wide, cols), 1)
    plane = m // SUB
    p_in[...] = jnp.where((m - plane * SUB) * planes + plane - 1 == j, 1.0, 0.0).astype(BF16)
    m = lax.broadcasted_iota(jnp.int32, (cols, cols), 0)
    j = lax.broadcasted_iota(jnp.int32, (cols, cols), 1)
    plane = j // SUB
    p_out[...] = jnp.where((j - plane * SUB) * planes + plane == m, 1.0, 0.0).astype(BF16)

    enc = Exchange(
        0, h, edges_enc, recv_enc, *[x_enc.at[i, 1 : planes + 1] for i in (1, h, 0, h + 1)]
    )
    pool = Exchange(
        1, hc, edges_pool, recv_pool, *[x_pool.at[i, 1 : cplanes + 1] for i in (1, hc, 0, hc + 1)]
    )
    skip = Exchange(
        2, h, edges_skip, recv_skip, *[x_skip.at[i, 1 : planes + 1] for i in (1, h, 0, h + 1)]
    )
    low = Exchange(3, hc, edges_coarse, recv_coarse, *[coarse.at[i] for i in (1, hc, 0, hc + 1)])

    loads[0].wait()
    for r in range(cycles):
        for i in range(h):
            edge_tmp[0, 2 * r, i : i + 1, :] = fields[r, i, 0:SUB, :].astype(F32)[0:1]
            edge_tmp[0, 2 * r + 1, i : i + 1, :] = fields[r, i, cols - SUB : cols, :].astype(F32)[SUB - 1 : SUB]
    enc.publish()

    def to_planes(i):
        for r in range(cycles):
            row = jnp.dot(p_in[...], fields[r, i], preferred_element_type=F32)
            x_enc[i + 1, :, r] = row.astype(BF16).reshape(planes + 2, SUB, ch)

    steps(0, h, 2, to_planes)
    pl.semaphore_wait(barrier, tiles - 1)
    enc.send_seams()
    enc.send_rows()

    loads[1].wait()

    def enc_row(i):
        value = conv(x_enc, i, 1, planes, enc_w[...].reshape(9 * ch, ch))[0] + enc_b[...]
        keep_ends(0, i, value)
        put_row(x_skip, i + 1, gelu_tanh(value))

    steps(1, h - 1, 3, enc_row)
    halo_row(x_enc, 0, planes, enc.wait_above, top_face)
    halo_row(x_enc, h + 1, planes, enc.wait_below, bottom_face)
    enc_row(0)
    enc_row(h - 1)
    enc.wait_seams()
    enc.load_seams()
    fix_ends(
        0,
        skip,
        h,
        lambda side: seam_term(0, side, enc_w[:, 2 * side].reshape(3 * ch, ch)),
        lambda i, side, r: x_skip.at[i + 1, planes if side else 1, r],
    )

    for q in range(hc):
        parts = []
        for k in range(cplanes):
            total = None
            for a in range(2):
                for b in range(2):
                    term = x_skip[2 * q + a + 1, 2 * k + b + 1].astype(F32)
                    total = term if total is None else total + term
            parts.append((total * 0.25)[None])
        value = jnp.concatenate(parts, axis=0)
        put_row(x_pool, q + 1, value)
        for r in range(cycles):
            edge_tmp[1, 2 * r, q : q + 1, :] = value[0, r, 0:1, :]
            edge_tmp[1, 2 * r + 1, q : q + 1, :] = value[-1, r, SUB - 1 : SUB, :]
    pool.publish()
    pool.send_seams()
    pool.send_rows()
    skip.publish()
    skip.send_seams()
    skip.send_rows()

    loads[2].wait()

    def dec_weights(part):
        picked = [dec_w[a, b, part * ch : (part + 1) * ch, :] for a in range(3) for b in range(3)]
        return jnp.concatenate(picked, axis=0)

    def dec_side(part, side):
        picked = [dec_w[a, 2 * side, part * ch : (part + 1) * ch, :] for a in range(3)]
        return jnp.concatenate(picked, axis=0)

    def dec_skip_row(i):
        acc_dec[i] = conv(x_skip, i, 1, planes, dec_weights(1))[0]

    steps(1, h - 1, 3, dec_skip_row)

    loads[3].wait()
    loads[4].wait()

    def mid_rows(i, n):
        value = conv(x_pool, i, n, cplanes, mid_w[...].reshape(9 * ch, ch)) + mid_b[...]
        for u in range(n):
            keep_ends(1, i + u, value[u])
        coarse[pl.ds(i + 1, n)] = gelu_tanh(value).astype(BF16)

    mid_rows(1, hc - 2)
    halo_row(x_pool, 0, cplanes, pool.wait_above, top_face)
    halo_row(x_pool, hc + 1, cplanes, pool.wait_below, bottom_face)
    mid_rows(0, 1)
    mid_rows(hc - 1, 1)
    pool.wait_seams()
    pool.load_seams()
    fix_ends(
        1,
        low,
        hc,
        lambda side: seam_term(1, side, mid_w[:, 2 * side].reshape(3 * ch, ch)),
        lambda i, side, r: coarse.at[i + 1, cplanes - 1 if side else 0, r],
    )
    low.publish()
    low.send_seams()
    low.send_rows()

    def up_rows(q, first, last):
        lhs = coarse[q].reshape(cplanes * cycles * SUB, ch)
        weight = jnp.concatenate([up_w[a, b] for a in range(first, last) for b in range(2)], axis=1)
        product = jnp.dot(lhs, weight, preferred_element_type=F32)
        for a in range(first, last):
            row = [None] * planes
            for b in range(2):
                at = (2 * (a - first) + b) * ch
                value = (product[:, at : at + ch] + up_b[...]).reshape(cplanes, cycles, SUB, ch)
                for k in range(cplanes):
                    row[2 * k + b] = value[k : k + 1]
            put_row(x_up, 2 * q + a - 1, jnp.concatenate(row, axis=0))

    for q in range(hc):
        up_rows(q + 1, 0, 2)

    def dec_up_row(i):
        value = acc_dec[i] + conv(x_up, i, 1, planes, dec_weights(0))[0] + dec_b[...]
        keep_ends(2, i, value)
        value = value.astype(BF16)
        for r in range(cycles):
            row = jnp.dot(p_out[...], value[:, r].reshape(cols, ch), preferred_element_type=F32)
            out[r, i] = row.astype(BF16)

    steps(1, h - 1, 3, dec_up_row)
    halo_row(x_skip, 0, planes, skip.wait_above, top_face)
    halo_row(x_skip, h + 1, planes, skip.wait_below, bottom_face)
    dec_skip_row(0)
    dec_skip_row(h - 1)
    skip.wait_seams()
    skip.load_seams()
    for side in range(2):
        terms[side] = seam_term(2, side, dec_side(1, side))

    for ex in (enc, pool, skip):
        ex.wait_sends()
    for row, q, a, missing, wait in (
        (0, 0, 1, top_face, low.wait_above),
        (h + 1, hc + 1, 0, bottom_face, low.wait_below),
    ):

        @pl.when(missing)
        def _():
            x_up[row] = jnp.zeros(x_up.shape[1:], BF16)

        @pl.when(jnp.logical_not(missing))
        def _():
            wait()
            up_rows(q, a, a + 1)

    dec_up_row(0)
    dec_up_row(h - 1)

    low.wait_seams()
    low.load_seams()
    lhs = jnp.concatenate([seam_tmp[3, side, r, 0:8, :] for side in range(2) for r in range(cycles)], axis=0)
    weight = jnp.concatenate([up_w[a, b] for a in range(2) for b in range(2)], axis=1)
    product = jnp.dot(lhs.astype(BF16), weight, preferred_element_type=F32)
    for side in range(2):
        for r in range(cycles):
            code = seam_code[side, r]
            last = lax.rem(code, 2) == 1
            mirrored = code >= 2
            at = 8 * (side * cycles + r)
            phases = []
            for a in range(2):
                pair = [product[at : at + 8, (2 * a + b) * ch : (2 * a + b + 1) * ch] for b in range(2)]
                phases.append(jnp.where(last, pair[1], pair[0]) + up_b[...])
            even = jnp.where(mirrored, phases[1], phases[0])
            odd = jnp.where(mirrored, phases[0], phases[1])
            seam_tmp[4, side, r, 0:1, :] = jnp.where(top_face, 0.0, odd[0:1])
            for k in range(hc):
                seam_tmp[4, side, r, 2 * k + 1 : 2 * k + 2, :] = even[k + 1 : k + 2]
                seam_tmp[4, side, r, 2 * k + 2 : 2 * k + 3, :] = odd[k + 1 : k + 2]
            seam_tmp[4, side, r, h + 1 : h + 2, :] = jnp.where(bottom_face, 0.0, even[hc + 1 : hc + 2])
    for side in range(2):
        pixels[side] = pre[2, side] + terms[side] + seam_term(4, side, dec_side(0, side))
    for side in range(2):
        lo = side * (cols - SUB)
        for r in range(cycles):
            for i in range(h):
                row = pixels[side, 8 * r + i : 8 * r + i + 1, :]
                tile = out[r, i, lo : lo + SUB, :].astype(F32)
                out[r, i, lo : lo + SUB, :] = jnp.where(at_sub == side * (SUB - 1), row, tile).astype(BF16)

    low.wait_sends()


def solution(mesh):
    tiles = mesh.shape["tile"]

    def on_device(fields, seam_tile, seam_code, enc_w, enc_b, mid_w, mid_b, up_w, up_b, dec_w, dec_b):
        cycles, h, cols, ch = fields.shape
        hc = h // 2
        planes = cols // SUB
        cplanes = planes // 2
        vmem = pl.BlockSpec(memory_space=pltpu.VMEM)
        smem = pl.BlockSpec(memory_space=pltpu.SMEM)
        hbm = pl.BlockSpec(memory_space=pl.ANY)
        ends = 2 * cycles
        slots = 2 * FACES
        return pl.pallas_call(
            functools.partial(kernel, tiles),
            out_shape=jax.ShapeDtypeStruct(fields.shape, BF16),
            in_specs=[smem, smem] + [hbm] * 5 + [vmem] * 4,
            out_specs=vmem,
            scratch_shapes=[
                pltpu.VMEM(fields.shape, BF16),
                pltpu.VMEM(enc_w.shape, BF16),
                pltpu.VMEM(mid_w.shape, BF16),
                pltpu.VMEM(up_w.shape, BF16),
                pltpu.VMEM(dec_w.shape, BF16),
                pltpu.VMEM((h + 2, planes + 2, cycles, SUB, ch), BF16),
                pltpu.VMEM((h + 2, planes + 2, cycles, SUB, ch), BF16),
                pltpu.VMEM((hc + 2, cplanes + 2, cycles, SUB, ch), BF16),
                pltpu.VMEM((h + 2, planes + 2, cycles, SUB, ch), BF16),
                pltpu.VMEM((hc + 2, cplanes, cycles, SUB, ch), BF16),
                pltpu.VMEM((h, planes, cycles, SUB, ch), F32),
                pltpu.VMEM((3, 2, 8 * cycles, ch), F32),
                pltpu.VMEM((2, 8 * cycles, ch), F32),
                pltpu.VMEM((2, 8 * cycles, ch), F32),
                pltpu.VMEM(((planes + 2) * SUB, cols), BF16),
                pltpu.VMEM((cols, cols), BF16),
                pltpu.VMEM((4, ends, 8, ch), F32),
                pltpu.VMEM((4, 2, 8, ch), F32),
                pltpu.VMEM((5, 2, cycles, 16, ch), F32),
                pltpu.VMEM((4, 2, 8, ch), BF16),
                pltpu.VMEM((ends, h, ch), BF16),
                pltpu.VMEM((ends, hc, ch), BF16),
                pltpu.VMEM((ends, h, ch), BF16),
                pltpu.VMEM((ends, hc, ch), BF16),
                pltpu.VMEM((slots, ends, h, ch), BF16),
                pltpu.VMEM((slots, ends, hc, ch), BF16),
                pltpu.VMEM((slots, ends, h, ch), BF16),
                pltpu.VMEM((slots, ends, hc, ch), BF16),
                pltpu.VMEM((2, slots, 8, ch), BF16),
                pltpu.VMEM((2, slots, 8, ch), BF16),
                pltpu.VMEM((2, slots, 8, ch), BF16),
                pltpu.VMEM((2, slots, 8, ch), BF16),
                pltpu.SemaphoreType.DMA((5,)),
                pltpu.SemaphoreType.DMA((4, 5)),
                pltpu.SemaphoreType.DMA((4, 5)),
            ],
            compiler_params=pltpu.CompilerParams(
                collective_id=0, has_side_effects=True, vmem_limit_bytes=60 * 1024 * 1024
            ),
        )(
            jnp.transpose(seam_tile, (1, 2, 0)).reshape(2, cycles),
            jnp.transpose(seam_code, (1, 2, 0)).reshape(2, cycles),
            fields,
            enc_w,
            mid_w,
            up_w,
            dec_w,
            enc_b.reshape(1, ch),
            mid_b.reshape(1, ch),
            up_b.reshape(1, ch),
            dec_b.reshape(1, ch),
        )

    return jax.shard_map(
        on_device,
        mesh=mesh,
        in_specs=(P("grp", "tile", None, None), P(None, "tile", None), P(None, "tile", None)) + (P(),) * 8,
        out_specs=P("grp", "tile", None, None),
        check_vma=False,
    )
```

```python
import functools

import jax
import jax.numpy as jnp
from jax import lax
from jax.experimental import pallas as pl
from jax.experimental.pallas import tpu as pltpu
from jax.sharding import PartitionSpec as P

F32 = jnp.float32
BF16 = jnp.bfloat16
FACES = 4
SUB = 16


def gelu_tanh(x):
    return 0.5 * x * (1.0 + jnp.tanh(0.7978845608 * (x + 0.044715 * (x * x * x))))


def kernel(
    tiles,
    seam_tile,
    seam_code,
    fields_hbm,
    enc_w_hbm,
    mid_w_hbm,
    up_w_hbm,
    dec_w_hbm,
    enc_b,
    mid_b,
    up_b,
    dec_b,
    out,
    fields,
    enc_w,
    mid_w,
    up_w,
    dec_w,
    x_enc,
    x_skip,
    x_pool,
    x_up,
    coarse,
    acc_dec,
    pre,
    pixels,
    terms,
    p_in,
    p_out,
    edge_tmp,
    corner_tmp,
    seam_tmp,
    corner_src,
    edges_enc,
    edges_pool,
    edges_skip,
    edges_coarse,
    recv_enc,
    recv_pool,
    recv_skip,
    recv_coarse,
    corner_enc,
    corner_pool,
    corner_skip,
    corner_coarse,
    load_sem,
    send_sem,
    recv_sem,
):
    recv_corners = (corner_enc, corner_pool, corner_skip, corner_coarse)
    cycles, h, cols, ch = fields.shape
    hc = h // 2
    planes = cols // SUB
    cplanes = planes // 2
    strips = tiles // FACES
    me = lax.axis_index("tile")
    place = lax.rem(me + strips // 2, tiles)
    face = place // strips
    strip = place - face * strips
    top_face = strip == 0
    bottom_face = strip == strips - 1
    has_above = strip > 0
    has_below = strip < strips - 1
    send_top = jnp.logical_and(has_above, strip != strips // 2)
    send_bottom = jnp.logical_and(has_below, strip != strips // 2 - 1)
    up_tile = lax.rem(me + tiles - 1, tiles)
    down_tile = lax.rem(me + 1, tiles)
    at_sub = lax.broadcasted_iota(jnp.int32, (SUB, ch), 0)

    def tile_of(f, s):
        return lax.rem(f * strips + s + tiles - strips // 2, tiles)

    faces = [lax.rem(face + j, FACES) for j in range(FACES)]

    loads = []
    for k, (src, dst) in enumerate(
        ((fields_hbm, fields), (enc_w_hbm, enc_w), (dec_w_hbm, dec_w), (mid_w_hbm, mid_w), (up_w_hbm, up_w))
    ):
        loads.append(pltpu.make_async_copy(src, dst, load_sem.at[k]))
    loads[0].start()

    barrier = pltpu.get_barrier_semaphore()

    @pl.loop(1, tiles)
    def _(k):
        pl.semaphore_signal(barrier, inc=1, device_id={"tile": lax.rem(me + k, tiles)})

    def remote(src, dst, e, send_at, recv_at, target):
        return pltpu.make_async_remote_copy(
            src_ref=src,
            dst_ref=dst,
            send_sem=send_sem.at[e, send_at],
            recv_sem=recv_sem.at[e, recv_at],
            device_id={"tile": target},
        )

    def shifted(value, last):
        if last:
            return jnp.where(at_sub == SUB - 1, 0.0, pltpu.roll(value, SUB - 1, 0)).astype(BF16)
        return jnp.where(at_sub == 0, 0.0, pltpu.roll(value, 1, 0)).astype(BF16)

    class Exchange:
        def __init__(self, e, rows, edge_ref, recv_ref, top, bottom, above, below):
            self.e, self.rows, self.edges, self.recv = e, rows, edge_ref, recv_ref
            self.top, self.bottom, self.above, self.below = top, bottom, above, below

        def publish(self):
            e, rows = self.e, self.rows
            value = edge_tmp[e, :, 0:rows, :].astype(BF16)
            self.edges[...] = value
            self.recv[face] = value
            for k in range(2 * cycles):
                corner_tmp[e, 0, k : k + 1, :] = edge_tmp[e, k, 0:1, :]
                corner_tmp[e, 1, k : k + 1, :] = edge_tmp[e, k, rows - 1 : rows, :]
            for which in range(2):
                corner_src[e, which] = corner_tmp[e, which].astype(BF16)

        def send_seams(self):
            e = self.e
            for kind in range(2):
                s = strip if kind == 0 else strips - 1 - strip
                for f in faces[1 - kind :]:
                    remote(self.edges, self.recv.at[kind * FACES + face], e, 2, 2, tile_of(f, s)).start()

            def corner(which, pos, kind, s):
                for f in faces:
                    dst = recv_corners[e].at[pos, kind * FACES + face]
                    remote(corner_src.at[e, which], dst, e, 3 + which, 3 + pos, tile_of(f, s)).start()

            @pl.when(send_bottom)
            def _():
                corner(1, 0, 0, strip + 1)
                corner(1, 1, 1, strips - 2 - strip)

            @pl.when(send_top)
            def _():
                corner(0, 1, 0, strip - 1)
                corner(0, 0, 1, strips - strip)

        def row_copies(self):
            return [
                (has_below, remote(self.bottom, self.above, self.e, 0, 0, down_tile)),
                (has_above, remote(self.top, self.below, self.e, 1, 1, up_tile)),
            ]

        def send_rows(self):
            for cond, copy in self.row_copies():
                pl.when(cond)(copy.start)

        def seam_wait(self):
            others = self.recv.at[pl.ds(0, 2 * FACES - 1)]
            return remote(others, others, self.e, 2, 2, up_tile)

        def corner_wait(self, at):
            whole = recv_corners[self.e].at[at]
            return remote(whole, whole, self.e, 3 + at, 3 + at, up_tile)

        def wait_sends(self):
            self.seam_wait().wait_send()
            pl.when(send_top)(self.corner_wait(0).wait_send)
            pl.when(send_bottom)(self.corner_wait(1).wait_send)
            for cond, copy in self.row_copies():
                pl.when(cond)(copy.wait_send)

        def wait_above(self):
            remote(self.bottom, self.above, self.e, 0, 0, down_tile).wait_recv()

        def wait_below(self):
            remote(self.top, self.below, self.e, 1, 1, up_tile).wait_recv()

        def wait_seams(self):
            self.seam_wait().wait_recv()
            pl.when(jnp.logical_and(has_above, strip != strips // 2))(self.corner_wait(0).wait_recv)
            pl.when(jnp.logical_and(has_below, strip != strips // 2 - 1))(self.corner_wait(1).wait_recv)

        def load_seams(self):
            rows, e = self.rows, self.e
            at = lax.broadcasted_iota(jnp.int32, (8, ch), 0)
            for side in range(2):
                for r in range(cycles):
                    partner, code = seam_tile[side, r], seam_code[side, r]
                    cycle = partner // tiles
                    home = lax.rem(partner - cycle * tiles + strips // 2, tiles) // strips
                    mirrored = code >= 2
                    slot = jnp.where(mirrored, FACES, 0) + home
                    k = 2 * cycle + lax.rem(code, 2)
                    column = self.recv[slot, k].astype(F32)
                    twin = self.recv[jnp.where(mirrored, 0, FACES) + home, k].astype(F32)
                    first, last = twin[0:1], twin[rows - 1 : rows]
                    ends = [recv_corners[e][pos, slot].astype(F32) for pos in range(2)]
                    above, below = [jnp.sum(jnp.where(at == k, end, 0.0), axis=0, keepdims=True) for end in ends]
                    above = jnp.where(strip == strips // 2, jnp.where(mirrored, first, last), above)
                    below = jnp.where(strip == strips // 2 - 1, jnp.where(mirrored, last, first), below)
                    seam_tmp[e, side, r, 0:1, :] = jnp.where(top_face, 0.0, above)
                    seam_tmp[e, side, r, rows + 1 : rows + 2, :] = jnp.where(bottom_face, 0.0, below)
                    for i in range(rows):
                        seam_tmp[e, side, r, i + 1 : i + 2, :] = jnp.where(
                            mirrored, column[rows - 1 - i : rows - i], column[i : i + 1]
                        )

    def seam_term(e, side, weight):
        lhs = [
            jnp.concatenate([seam_tmp[e, side, r, a : a + 8, :] for r in range(cycles)], axis=0) for a in range(3)
        ]
        return jnp.dot(jnp.concatenate(lhs, axis=1).astype(BF16), weight, preferred_element_type=F32)

    def conv(x, i, n, q, weight):
        taps = [
            x[pl.ds(i + a, n), b : b + q].reshape(n * q * cycles * SUB, ch) for a in range(3) for b in range(3)
        ]
        product = jnp.dot(jnp.concatenate(taps, axis=1), weight, preferred_element_type=F32)
        return product.reshape(n, q, cycles, SUB, ch)

    def keep_ends(stage, i, value):
        for r in range(cycles):
            pre[stage, 0, pl.ds(8 * r + i, 1), :] = value[0, r, 0:1, :]
            pre[stage, 1, pl.ds(8 * r + i, 1), :] = value[-1, r, SUB - 1 : SUB, :]

    def put_row(x, i, value):
        q = value.shape[0]
        x[i, 1 : q + 1] = value.astype(BF16)
        for r in range(cycles):
            x[i, 0, r] = shifted(value[q - 1, r], False)
            x[i, q + 1, r] = shifted(value[0, r], True)

    def halo_row(x, i, q, wait, missing):
        @pl.when(missing)
        def _():
            x[i] = jnp.zeros(x.shape[1:], BF16)

        @pl.when(jnp.logical_not(missing))
        def _():
            wait()
            for r in range(cycles):
                x[i, 0, r] = shifted(x[i, q, r].astype(F32), False)
                x[i, q + 1, r] = shifted(x[i, 1, r].astype(F32), True)

    def fix_ends(stage, ex, rows, term_of, tile_ref):
        for side in range(2):
            value = gelu_tanh(pre[stage, side] + term_of(side))
            pixels[side] = value
            for r in range(cycles):
                edge_tmp[ex.e, 2 * r + side, 0:rows, :] = value[8 * r : 8 * r + rows]
        for side in range(2):
            for r in range(cycles):
                for i in range(rows):
                    tile = tile_ref(i, side, r)
                    row = pixels[side, 8 * r + i : 8 * r + i + 1, :]
                    tile[...] = jnp.where(at_sub == side * (SUB - 1), row, tile[...].astype(F32)).astype(BF16)

    def steps(lo, hi, most, body):
        count = hi - lo
        unroll = max(u for u in range(1, most + 1) if count % u == 0)

        @pl.loop(0, count // unroll)
        def _(k):
            for u in range(unroll):
                body(lo + k * unroll + u)

    wide = (planes + 2) * SUB
    m = lax.broadcasted_iota(jnp.int32, (wide, cols), 0)
    j = lax.broadcasted_iota(jnp.int32, (wide, cols), 1)
    plane = m // SUB
    p_in[...] = jnp.where((m - plane * SUB) * planes + plane - 1 == j, 1.0, 0.0).astype(BF16)
    m = lax.broadcasted_iota(jnp.int32, (cols, cols), 0)
    j = lax.broadcasted_iota(jnp.int32, (cols, cols), 1)
    plane = j // SUB
    p_out[...] = jnp.where((j - plane * SUB) * planes + plane == m, 1.0, 0.0).astype(BF16)

    enc = Exchange(
        0, h, edges_enc, recv_enc, *[x_enc.at[i, 1 : planes + 1] for i in (1, h, 0, h + 1)]
    )
    pool = Exchange(
        1, hc, edges_pool, recv_pool, *[x_pool.at[i, 1 : cplanes + 1] for i in (1, hc, 0, hc + 1)]
    )
    skip = Exchange(
        2, h, edges_skip, recv_skip, *[x_skip.at[i, 1 : planes + 1] for i in (1, h, 0, h + 1)]
    )
    low = Exchange(3, hc, edges_coarse, recv_coarse, *[coarse.at[i] for i in (1, hc, 0, hc + 1)])

    loads[0].wait()
    loads[1].start()
    for r in range(cycles):
        for i in range(h):
            edge_tmp[0, 2 * r, i : i + 1, :] = fields[r, i, 0:SUB, :].astype(F32)[0:1]
            edge_tmp[0, 2 * r + 1, i : i + 1, :] = fields[r, i, cols - SUB : cols, :].astype(F32)[SUB - 1 : SUB]
    enc.publish()

    def to_planes(i):
        for r in range(cycles):
            row = jnp.dot(p_in[...], fields[r, i], preferred_element_type=F32)
            x_enc[i + 1, :, r] = row.astype(BF16).reshape(planes + 2, SUB, ch)

    steps(0, h, 2, to_planes)
    pl.semaphore_wait(barrier, tiles - 1)
    enc.send_seams()
    enc.send_rows()

    loads[1].wait()
    for copy in loads[2:]:
        copy.start()

    def enc_row(i):
        value = conv(x_enc, i, 1, planes, enc_w[...].reshape(9 * ch, ch))[0] + enc_b[...]
        keep_ends(0, i, value)
        put_row(x_skip, i + 1, gelu_tanh(value))

    steps(1, h - 1, 3, enc_row)
    halo_row(x_enc, 0, planes, enc.wait_above, top_face)
    halo_row(x_enc, h + 1, planes, enc.wait_below, bottom_face)
    enc_row(0)
    enc_row(h - 1)
    enc.wait_seams()
    enc.load_seams()
    fix_ends(
        0,
        skip,
        h,
        lambda side: seam_term(0, side, enc_w[:, 2 * side].reshape(3 * ch, ch)),
        lambda i, side, r: x_skip.at[i + 1, planes if side else 1, r],
    )

    for q in range(hc):
        parts = []
        for k in range(cplanes):
            total = None
            for a in range(2):
                for b in range(2):
                    term = x_skip[2 * q + a + 1, 2 * k + b + 1].astype(F32)
                    total = term if total is None else total + term
            parts.append((total * 0.25)[None])
        value = jnp.concatenate(parts, axis=0)
        put_row(x_pool, q + 1, value)
        for r in range(cycles):
            edge_tmp[1, 2 * r, q : q + 1, :] = value[0, r, 0:1, :]
            edge_tmp[1, 2 * r + 1, q : q + 1, :] = value[-1, r, SUB - 1 : SUB, :]
    pool.publish()
    pool.send_seams()
    pool.send_rows()

    loads[2].wait()

    def dec_weights(part):
        picked = [dec_w[a, b, part * ch : (part + 1) * ch, :] for a in range(3) for b in range(3)]
        return jnp.concatenate(picked, axis=0)

    def dec_side(part, side):
        picked = [dec_w[a, 2 * side, part * ch : (part + 1) * ch, :] for a in range(3)]
        return jnp.concatenate(picked, axis=0)

    def dec_skip_row(i):
        acc_dec[i] = conv(x_skip, i, 1, planes, dec_weights(1))[0]

    steps(1, h - 1, 3, dec_skip_row)
    skip.publish()
    skip.send_seams()
    skip.send_rows()

    loads[3].wait()
    loads[4].wait()

    def mid_rows(i, n):
        value = conv(x_pool, i, n, cplanes, mid_w[...].reshape(9 * ch, ch)) + mid_b[...]
        for u in range(n):
            keep_ends(1, i + u, value[u])
        coarse[pl.ds(i + 1, n)] = gelu_tanh(value).astype(BF16)

    mid_rows(1, hc - 2)
    halo_row(x_pool, 0, cplanes, pool.wait_above, top_face)
    halo_row(x_pool, hc + 1, cplanes, pool.wait_below, bottom_face)
    mid_rows(0, 1)
    mid_rows(hc - 1, 1)
    pool.wait_seams()
    pool.load_seams()
    fix_ends(
        1,
        low,
        hc,
        lambda side: seam_term(1, side, mid_w[:, 2 * side].reshape(3 * ch, ch)),
        lambda i, side, r: coarse.at[i + 1, cplanes - 1 if side else 0, r],
    )
    low.publish()
    low.send_seams()
    low.send_rows()

    def up_rows(q, first, last):
        lhs = coarse[q].reshape(cplanes * cycles * SUB, ch)
        weight = jnp.concatenate([up_w[a, b] for a in range(first, last) for b in range(2)], axis=1)
        product = jnp.dot(lhs, weight, preferred_element_type=F32)
        for a in range(first, last):
            row = [None] * planes
            for b in range(2):
                at = (2 * (a - first) + b) * ch
                value = (product[:, at : at + ch] + up_b[...]).reshape(cplanes, cycles, SUB, ch)
                for k in range(cplanes):
                    row[2 * k + b] = value[k : k + 1]
            put_row(x_up, 2 * q + a - 1, jnp.concatenate(row, axis=0))

    for q in range(hc):
        up_rows(q + 1, 0, 2)

    def dec_up_row(i):
        value = acc_dec[i] + conv(x_up, i, 1, planes, dec_weights(0))[0] + dec_b[...]
        keep_ends(2, i, value)
        value = value.astype(BF16)
        for r in range(cycles):
            row = jnp.dot(p_out[...], value[:, r].reshape(cols, ch), preferred_element_type=F32)
            out[r, i] = row.astype(BF16)

    steps(1, h - 1, 3, dec_up_row)
    halo_row(x_skip, 0, planes, skip.wait_above, top_face)
    halo_row(x_skip, h + 1, planes, skip.wait_below, bottom_face)
    dec_skip_row(0)
    dec_skip_row(h - 1)
    skip.wait_seams()
    skip.load_seams()
    for side in range(2):
        terms[side] = seam_term(2, side, dec_side(1, side))

    for ex in (enc, pool, skip):
        ex.wait_sends()
    for row, q, a, missing, wait in (
        (0, 0, 1, top_face, low.wait_above),
        (h + 1, hc + 1, 0, bottom_face, low.wait_below),
    ):

        @pl.when(missing)
        def _():
            x_up[row] = jnp.zeros(x_up.shape[1:], BF16)

        @pl.when(jnp.logical_not(missing))
        def _():
            wait()
            up_rows(q, a, a + 1)

    dec_up_row(0)
    dec_up_row(h - 1)

    low.wait_seams()
    low.load_seams()
    lhs = jnp.concatenate([seam_tmp[3, side, r, 0:8, :] for side in range(2) for r in range(cycles)], axis=0)
    weight = jnp.concatenate([up_w[a, b] for a in range(2) for b in range(2)], axis=1)
    product = jnp.dot(lhs.astype(BF16), weight, preferred_element_type=F32)
    for side in range(2):
        for r in range(cycles):
            code = seam_code[side, r]
            last = lax.rem(code, 2) == 1
            mirrored = code >= 2
            at = 8 * (side * cycles + r)
            phases = []
            for a in range(2):
                pair = [product[at : at + 8, (2 * a + b) * ch : (2 * a + b + 1) * ch] for b in range(2)]
                phases.append(jnp.where(last, pair[1], pair[0]) + up_b[...])
            even = jnp.where(mirrored, phases[1], phases[0])
            odd = jnp.where(mirrored, phases[0], phases[1])
            seam_tmp[4, side, r, 0:1, :] = jnp.where(top_face, 0.0, odd[0:1])
            for k in range(hc):
                seam_tmp[4, side, r, 2 * k + 1 : 2 * k + 2, :] = even[k + 1 : k + 2]
                seam_tmp[4, side, r, 2 * k + 2 : 2 * k + 3, :] = odd[k + 1 : k + 2]
            seam_tmp[4, side, r, h + 1 : h + 2, :] = jnp.where(bottom_face, 0.0, even[hc + 1 : hc + 2])
    for side in range(2):
        pixels[side] = pre[2, side] + terms[side] + seam_term(4, side, dec_side(0, side))
    for side in range(2):
        lo = side * (cols - SUB)
        for r in range(cycles):
            for i in range(h):
                row = pixels[side, 8 * r + i : 8 * r + i + 1, :]
                tile = out[r, i, lo : lo + SUB, :].astype(F32)
                out[r, i, lo : lo + SUB, :] = jnp.where(at_sub == side * (SUB - 1), row, tile).astype(BF16)

    low.wait_sends()


def solution(mesh):
    tiles = mesh.shape["tile"]

    def on_device(fields, seam_tile, seam_code, enc_w, enc_b, mid_w, mid_b, up_w, up_b, dec_w, dec_b):
        cycles, h, cols, ch = fields.shape
        hc = h // 2
        planes = cols // SUB
        cplanes = planes // 2
        vmem = pl.BlockSpec(memory_space=pltpu.VMEM)
        smem = pl.BlockSpec(memory_space=pltpu.SMEM)
        hbm = pl.BlockSpec(memory_space=pl.ANY)
        ends = 2 * cycles
        slots = 2 * FACES
        operands = [
            pltpu.with_memory_space_constraint(x, pltpu.HBM)
            for x in (
                jnp.transpose(seam_tile, (1, 2, 0)).reshape(2, cycles),
                jnp.transpose(seam_code, (1, 2, 0)).reshape(2, cycles),
                fields,
                enc_w,
                mid_w,
                up_w,
                dec_w,
                enc_b.reshape(1, ch),
                mid_b.reshape(1, ch),
                up_b.reshape(1, ch),
                dec_b.reshape(1, ch),
            )
        ]
        return pl.pallas_call(
            functools.partial(kernel, tiles),
            out_shape=jax.ShapeDtypeStruct(fields.shape, BF16),
            in_specs=[smem, smem] + [hbm] * 5 + [vmem] * 4,
            out_specs=vmem,
            scratch_shapes=[
                pltpu.VMEM(fields.shape, BF16),
                pltpu.VMEM(enc_w.shape, BF16),
                pltpu.VMEM(mid_w.shape, BF16),
                pltpu.VMEM(up_w.shape, BF16),
                pltpu.VMEM(dec_w.shape, BF16),
                pltpu.VMEM((h + 2, planes + 2, cycles, SUB, ch), BF16),
                pltpu.VMEM((h + 2, planes + 2, cycles, SUB, ch), BF16),
                pltpu.VMEM((hc + 2, cplanes + 2, cycles, SUB, ch), BF16),
                pltpu.VMEM((h + 2, planes + 2, cycles, SUB, ch), BF16),
                pltpu.VMEM((hc + 2, cplanes, cycles, SUB, ch), BF16),
                pltpu.VMEM((h, planes, cycles, SUB, ch), F32),
                pltpu.VMEM((3, 2, 8 * cycles, ch), F32),
                pltpu.VMEM((2, 8 * cycles, ch), F32),
                pltpu.VMEM((2, 8 * cycles, ch), F32),
                pltpu.VMEM(((planes + 2) * SUB, cols), BF16),
                pltpu.VMEM((cols, cols), BF16),
                pltpu.VMEM((4, ends, 8, ch), F32),
                pltpu.VMEM((4, 2, 8, ch), F32),
                pltpu.VMEM((5, 2, cycles, 16, ch), F32),
                pltpu.VMEM((4, 2, 8, ch), BF16),
                pltpu.VMEM((ends, h, ch), BF16),
                pltpu.VMEM((ends, hc, ch), BF16),
                pltpu.VMEM((ends, h, ch), BF16),
                pltpu.VMEM((ends, hc, ch), BF16),
                pltpu.VMEM((slots, ends, h, ch), BF16),
                pltpu.VMEM((slots, ends, hc, ch), BF16),
                pltpu.VMEM((slots, ends, h, ch), BF16),
                pltpu.VMEM((slots, ends, hc, ch), BF16),
                pltpu.VMEM((2, slots, 8, ch), BF16),
                pltpu.VMEM((2, slots, 8, ch), BF16),
                pltpu.VMEM((2, slots, 8, ch), BF16),
                pltpu.VMEM((2, slots, 8, ch), BF16),
                pltpu.SemaphoreType.DMA((5,)),
                pltpu.SemaphoreType.DMA((4, 5)),
                pltpu.SemaphoreType.DMA((4, 5)),
            ],
            compiler_params=pltpu.CompilerParams(
                collective_id=0, has_side_effects=True, vmem_limit_bytes=44 * 1024 * 1024
            ),
        )(*operands)

    return jax.shard_map(
        on_device,
        mesh=mesh,
        in_specs=(P("grp", "tile", None, None), P(None, "tile", None), P(None, "tile", None)) + (P(),) * 8,
        out_specs=P("grp", "tile", None, None),
        check_vma=False,
    )
```

```python
import functools

import jax
import jax.numpy as jnp
from jax import lax
from jax.experimental import pallas as pl
from jax.experimental.pallas import tpu as pltpu
from jax.sharding import PartitionSpec as P

F32 = jnp.float32
BF16 = jnp.bfloat16
FACES = 4
SUB = 16
RELAYED = (0, 1, 2, 3)


def gelu_tanh(x):
    return 0.5 * x * (1.0 + jnp.tanh(0.7978845608 * (x + 0.044715 * (x * x * x))))


def kernel(
    tiles,
    seam_tile,
    seam_code,
    fields_hbm,
    enc_w_hbm,
    mid_w_hbm,
    up_w_hbm,
    dec_w_hbm,
    enc_b,
    mid_b,
    up_b,
    dec_b,
    out,
    fields,
    enc_w,
    mid_w,
    up_w,
    dec_w,
    x_enc,
    x_skip,
    x_pool,
    x_up,
    coarse,
    acc_dec,
    pre,
    pixels,
    terms,
    p_in,
    p_out,
    edge_tmp,
    corner_tmp,
    seam_tmp,
    corner_src,
    edges_enc,
    edges_pool,
    edges_skip,
    edges_coarse,
    recv_enc,
    recv_pool,
    recv_skip,
    recv_coarse,
    corner_enc,
    corner_pool,
    corner_skip,
    corner_coarse,
    load_sem,
    send_sem,
    recv_sem,
):
    recv_corners = (corner_enc, corner_pool, corner_skip, corner_coarse)
    cycles, h, cols, ch = fields.shape
    hc = h // 2
    planes = cols // SUB
    cplanes = planes // 2
    strips = tiles // FACES
    me = lax.axis_index("tile")
    place = lax.rem(me + strips // 2, tiles)
    face = place // strips
    strip = place - face * strips
    top_face = strip == 0
    bottom_face = strip == strips - 1
    has_above = strip > 0
    has_below = strip < strips - 1
    send_top = jnp.logical_and(has_above, strip != strips // 2)
    send_bottom = jnp.logical_and(has_below, strip != strips // 2 - 1)
    up_tile = lax.rem(me + tiles - 1, tiles)
    down_tile = lax.rem(me + 1, tiles)
    at_sub = lax.broadcasted_iota(jnp.int32, (SUB, ch), 0)

    def tile_of(f, s):
        return lax.rem(f * strips + s + tiles - strips // 2, tiles)

    faces = [lax.rem(face + j, FACES) for j in range(FACES)]

    loads = []
    for k, (src, dst) in enumerate(
        ((fields_hbm, fields), (enc_w_hbm, enc_w), (dec_w_hbm, dec_w), (mid_w_hbm, mid_w), (up_w_hbm, up_w))
    ):
        loads.append(pltpu.make_async_copy(src, dst, load_sem.at[k]))
    loads[0].start()

    barrier = pltpu.get_barrier_semaphore()

    @pl.loop(1, tiles)
    def _(k):
        pl.semaphore_signal(barrier, inc=1, device_id={"tile": lax.rem(me + k, tiles)})

    def remote(src, dst, e, send_at, recv_at, target):
        return pltpu.make_async_remote_copy(
            src_ref=src,
            dst_ref=dst,
            send_sem=send_sem.at[e, send_at],
            recv_sem=recv_sem.at[e, recv_at],
            device_id={"tile": target},
        )

    def shifted(value, last):
        if last:
            return jnp.where(at_sub == SUB - 1, 0.0, pltpu.roll(value, SUB - 1, 0)).astype(BF16)
        return jnp.where(at_sub == 0, 0.0, pltpu.roll(value, 1, 0)).astype(BF16)

    class Exchange:
        def __init__(self, e, rows, edge_ref, recv_ref, top, bottom, above, below):
            self.e, self.rows, self.edges, self.recv = e, rows, edge_ref, recv_ref
            self.top, self.bottom, self.above, self.below = top, bottom, above, below

        def publish(self):
            e, rows = self.e, self.rows
            value = edge_tmp[e, :, 0:rows, :].astype(BF16)
            self.edges[...] = value
            self.recv[face] = value
            for k in range(2 * cycles):
                corner_tmp[e, 0, k : k + 1, :] = edge_tmp[e, k, 0:1, :]
                corner_tmp[e, 1, k : k + 1, :] = edge_tmp[e, k, rows - 1 : rows, :]
            for which in range(2):
                corner_src[e, which] = corner_tmp[e, which].astype(BF16)

        def send_seams(self):
            e = self.e
            for kind in range(1 if e in RELAYED else 2):
                s = strip if kind == 0 else strips - 1 - strip
                for f in faces[1 - kind :]:
                    remote(self.edges, self.recv.at[kind * FACES + face], e, 2, 2, tile_of(f, s)).start()

            def corner(which, pos, kind, s):
                for f in faces:
                    dst = recv_corners[e].at[pos, kind * FACES + face]
                    remote(corner_src.at[e, which], dst, e, 3 + which, 3 + pos, tile_of(f, s)).start()

            @pl.when(send_bottom)
            def _():
                corner(1, 0, 0, strip + 1)
                corner(1, 1, 1, strips - 2 - strip)

            @pl.when(send_top)
            def _():
                corner(0, 1, 0, strip - 1)
                corner(0, 0, 1, strips - strip)

        def row_copies(self):
            return [
                (has_below, remote(self.bottom, self.above, self.e, 0, 0, down_tile)),
                (has_above, remote(self.top, self.below, self.e, 1, 1, up_tile)),
            ]

        def send_rows(self):
            for cond, copy in self.row_copies():
                pl.when(cond)(copy.start)

        def seam_wait(self):
            others = self.recv.at[pl.ds(0, (FACES if self.e in RELAYED else 2 * FACES) - 1)]
            return remote(others, others, self.e, 2, 2, up_tile)

        def relay_copy(self):
            step = jnp.where(strip < strips // 2, FACES - 1, 1)
            twin = tile_of(lax.rem(face + step, FACES), strips - 1 - strip)
            return remote(
                self.recv.at[pl.ds(0, FACES)], self.recv.at[pl.ds(FACES, FACES)], self.e, 5, 5, twin
            )

        def relay(self):
            if self.e in RELAYED:
                self.seam_wait().wait_recv()
                self.relay_copy().start()

        def corner_wait(self, at):
            whole = recv_corners[self.e].at[at]
            return remote(whole, whole, self.e, 3 + at, 3 + at, up_tile)

        def wait_sends(self):
            self.seam_wait().wait_send()
            if self.e in RELAYED:
                self.relay_copy().wait_send()
            pl.when(send_top)(self.corner_wait(0).wait_send)
            pl.when(send_bottom)(self.corner_wait(1).wait_send)
            for cond, copy in self.row_copies():
                pl.when(cond)(copy.wait_send)

        def wait_above(self):
            remote(self.bottom, self.above, self.e, 0, 0, down_tile).wait_recv()

        def wait_below(self):
            remote(self.top, self.below, self.e, 1, 1, up_tile).wait_recv()

        def wait_seams(self):
            if self.e in RELAYED:
                self.relay_copy().wait_recv()
            else:
                self.seam_wait().wait_recv()
            pl.when(jnp.logical_and(has_above, strip != strips // 2))(self.corner_wait(0).wait_recv)
            pl.when(jnp.logical_and(has_below, strip != strips // 2 - 1))(self.corner_wait(1).wait_recv)

        def load_seams(self):
            rows, e = self.rows, self.e
            at = lax.broadcasted_iota(jnp.int32, (8, ch), 0)
            for side in range(2):
                for r in range(cycles):
                    partner, code = seam_tile[side, r], seam_code[side, r]
                    cycle = partner // tiles
                    home = lax.rem(partner - cycle * tiles + strips // 2, tiles) // strips
                    mirrored = code >= 2
                    slot = jnp.where(mirrored, FACES, 0) + home
                    k = 2 * cycle + lax.rem(code, 2)
                    column = self.recv[slot, k].astype(F32)
                    twin = self.recv[jnp.where(mirrored, 0, FACES) + home, k].astype(F32)
                    first, last = twin[0:1], twin[rows - 1 : rows]
                    ends = [recv_corners[e][pos, slot].astype(F32) for pos in range(2)]
                    above, below = [jnp.sum(jnp.where(at == k, end, 0.0), axis=0, keepdims=True) for end in ends]
                    above = jnp.where(strip == strips // 2, jnp.where(mirrored, first, last), above)
                    below = jnp.where(strip == strips // 2 - 1, jnp.where(mirrored, last, first), below)
                    seam_tmp[e, side, r, 0:1, :] = jnp.where(top_face, 0.0, above)
                    seam_tmp[e, side, r, rows + 1 : rows + 2, :] = jnp.where(bottom_face, 0.0, below)
                    for i in range(rows):
                        seam_tmp[e, side, r, i + 1 : i + 2, :] = jnp.where(
                            mirrored, column[rows - 1 - i : rows - i], column[i : i + 1]
                        )

    def seam_term(e, side, weight):
        lhs = [
            jnp.concatenate([seam_tmp[e, side, r, a : a + 8, :] for r in range(cycles)], axis=0) for a in range(3)
        ]
        return jnp.dot(jnp.concatenate(lhs, axis=1).astype(BF16), weight, preferred_element_type=F32)

    def conv(x, i, n, q, weight):
        taps = [
            x[pl.ds(i + a, n), b : b + q].reshape(n * q * cycles * SUB, ch) for a in range(3) for b in range(3)
        ]
        product = jnp.dot(jnp.concatenate(taps, axis=1), weight, preferred_element_type=F32)
        return product.reshape(n, q, cycles, SUB, ch)

    def keep_ends(stage, i, value):
        for r in range(cycles):
            pre[stage, 0, pl.ds(8 * r + i, 1), :] = value[0, r, 0:1, :]
            pre[stage, 1, pl.ds(8 * r + i, 1), :] = value[-1, r, SUB - 1 : SUB, :]

    def put_row(x, i, value):
        q = value.shape[0]
        x[i, 1 : q + 1] = value.astype(BF16)
        for r in range(cycles):
            x[i, 0, r] = shifted(value[q - 1, r], False)
            x[i, q + 1, r] = shifted(value[0, r], True)

    def halo_row(x, i, q, wait, missing):
        @pl.when(missing)
        def _():
            x[i] = jnp.zeros(x.shape[1:], BF16)

        @pl.when(jnp.logical_not(missing))
        def _():
            wait()
            for r in range(cycles):
                x[i, 0, r] = shifted(x[i, q, r].astype(F32), False)
                x[i, q + 1, r] = shifted(x[i, 1, r].astype(F32), True)

    def fix_ends(stage, ex, rows, term_of, tile_ref):
        for side in range(2):
            value = gelu_tanh(pre[stage, side] + term_of(side))
            pixels[side] = value
            for r in range(cycles):
                edge_tmp[ex.e, 2 * r + side, 0:rows, :] = value[8 * r : 8 * r + rows]
        for side in range(2):
            for r in range(cycles):
                for i in range(rows):
                    tile = tile_ref(i, side, r)
                    row = pixels[side, 8 * r + i : 8 * r + i + 1, :]
                    tile[...] = jnp.where(at_sub == side * (SUB - 1), row, tile[...].astype(F32)).astype(BF16)

    def steps(lo, hi, most, body):
        count = hi - lo
        unroll = max(u for u in range(1, most + 1) if count % u == 0)

        @pl.loop(0, count // unroll)
        def _(k):
            for u in range(unroll):
                body(lo + k * unroll + u)

    wide = (planes + 2) * SUB
    m = lax.broadcasted_iota(jnp.int32, (wide, cols), 0)
    j = lax.broadcasted_iota(jnp.int32, (wide, cols), 1)
    plane = m // SUB
    p_in[...] = jnp.where((m - plane * SUB) * planes + plane - 1 == j, 1.0, 0.0).astype(BF16)
    m = lax.broadcasted_iota(jnp.int32, (cols, cols), 0)
    j = lax.broadcasted_iota(jnp.int32, (cols, cols), 1)
    plane = j // SUB
    p_out[...] = jnp.where((j - plane * SUB) * planes + plane == m, 1.0, 0.0).astype(BF16)

    enc = Exchange(
        0, h, edges_enc, recv_enc, *[x_enc.at[i, 1 : planes + 1] for i in (1, h, 0, h + 1)]
    )
    pool = Exchange(
        1, hc, edges_pool, recv_pool, *[x_pool.at[i, 1 : cplanes + 1] for i in (1, hc, 0, hc + 1)]
    )
    skip = Exchange(
        2, h, edges_skip, recv_skip, *[x_skip.at[i, 1 : planes + 1] for i in (1, h, 0, h + 1)]
    )
    low = Exchange(3, hc, edges_coarse, recv_coarse, *[coarse.at[i] for i in (1, hc, 0, hc + 1)])

    loads[0].wait()
    loads[1].start()
    for r in range(cycles):
        for i in range(h):
            edge_tmp[0, 2 * r, i : i + 1, :] = fields[r, i, 0:SUB, :].astype(F32)[0:1]
            edge_tmp[0, 2 * r + 1, i : i + 1, :] = fields[r, i, cols - SUB : cols, :].astype(F32)[SUB - 1 : SUB]
    enc.publish()

    def to_planes(i):
        for r in range(cycles):
            row = jnp.dot(p_in[...], fields[r, i], preferred_element_type=F32)
            x_enc[i + 1, :, r] = row.astype(BF16).reshape(planes + 2, SUB, ch)

    steps(0, h, 2, to_planes)
    pl.semaphore_wait(barrier, tiles - 1)
    enc.send_seams()
    enc.send_rows()

    loads[1].wait()
    for copy in loads[2:]:
        copy.start()

    def enc_row(i):
        value = conv(x_enc, i, 1, planes, enc_w[...].reshape(9 * ch, ch))[0] + enc_b[...]
        keep_ends(0, i, value)
        put_row(x_skip, i + 1, gelu_tanh(value))

    steps(1, h - 1, 3, enc_row)
    enc.relay()
    halo_row(x_enc, 0, planes, enc.wait_above, top_face)
    halo_row(x_enc, h + 1, planes, enc.wait_below, bottom_face)
    enc_row(0)
    enc_row(h - 1)
    enc.wait_seams()
    enc.load_seams()
    fix_ends(
        0,
        skip,
        h,
        lambda side: seam_term(0, side, enc_w[:, 2 * side].reshape(3 * ch, ch)),
        lambda i, side, r: x_skip.at[i + 1, planes if side else 1, r],
    )

    for q in range(hc):
        parts = []
        for k in range(cplanes):
            total = None
            for a in range(2):
                for b in range(2):
                    term = x_skip[2 * q + a + 1, 2 * k + b + 1].astype(F32)
                    total = term if total is None else total + term
            parts.append((total * 0.25)[None])
        value = jnp.concatenate(parts, axis=0)
        put_row(x_pool, q + 1, value)
        for r in range(cycles):
            edge_tmp[1, 2 * r, q : q + 1, :] = value[0, r, 0:1, :]
            edge_tmp[1, 2 * r + 1, q : q + 1, :] = value[-1, r, SUB - 1 : SUB, :]
    pool.publish()
    pool.send_seams()
    pool.send_rows()

    loads[2].wait()

    def dec_weights(part):
        picked = [dec_w[a, b, part * ch : (part + 1) * ch, :] for a in range(3) for b in range(3)]
        return jnp.concatenate(picked, axis=0)

    def dec_side(part, side):
        picked = [dec_w[a, 2 * side, part * ch : (part + 1) * ch, :] for a in range(3)]
        return jnp.concatenate(picked, axis=0)

    def dec_skip_row(i):
        acc_dec[i] = conv(x_skip, i, 1, planes, dec_weights(1))[0]

    steps(1, h - 1, 3, dec_skip_row)
    pool.relay()
    skip.publish()
    skip.send_seams()
    skip.send_rows()

    loads[3].wait()
    loads[4].wait()

    def mid_rows(i, n):
        value = conv(x_pool, i, n, cplanes, mid_w[...].reshape(9 * ch, ch)) + mid_b[...]
        for u in range(n):
            keep_ends(1, i + u, value[u])
        coarse[pl.ds(i + 1, n)] = gelu_tanh(value).astype(BF16)

    mid_rows(1, hc - 2)
    halo_row(x_pool, 0, cplanes, pool.wait_above, top_face)
    halo_row(x_pool, hc + 1, cplanes, pool.wait_below, bottom_face)
    mid_rows(0, 1)
    mid_rows(hc - 1, 1)
    pool.wait_seams()
    pool.load_seams()
    fix_ends(
        1,
        low,
        hc,
        lambda side: seam_term(1, side, mid_w[:, 2 * side].reshape(3 * ch, ch)),
        lambda i, side, r: coarse.at[i + 1, cplanes - 1 if side else 0, r],
    )
    low.publish()
    low.send_seams()
    low.send_rows()

    skip.relay()

    def up_rows(q, first, last):
        lhs = coarse[q].reshape(cplanes * cycles * SUB, ch)
        weight = jnp.concatenate([up_w[a, b] for a in range(first, last) for b in range(2)], axis=1)
        product = jnp.dot(lhs, weight, preferred_element_type=F32)
        for a in range(first, last):
            row = [None] * planes
            for b in range(2):
                at = (2 * (a - first) + b) * ch
                value = (product[:, at : at + ch] + up_b[...]).reshape(cplanes, cycles, SUB, ch)
                for k in range(cplanes):
                    row[2 * k + b] = value[k : k + 1]
            put_row(x_up, 2 * q + a - 1, jnp.concatenate(row, axis=0))

    for q in range(hc):
        up_rows(q + 1, 0, 2)

    def dec_up_row(i):
        value = acc_dec[i] + conv(x_up, i, 1, planes, dec_weights(0))[0] + dec_b[...]
        keep_ends(2, i, value)
        value = value.astype(BF16)
        for r in range(cycles):
            row = jnp.dot(p_out[...], value[:, r].reshape(cols, ch), preferred_element_type=F32)
            out[r, i] = row.astype(BF16)

    steps(1, h - 1, 3, dec_up_row)
    low.relay()
    halo_row(x_skip, 0, planes, skip.wait_above, top_face)
    halo_row(x_skip, h + 1, planes, skip.wait_below, bottom_face)
    dec_skip_row(0)
    dec_skip_row(h - 1)
    skip.wait_seams()
    skip.load_seams()
    for side in range(2):
        terms[side] = seam_term(2, side, dec_side(1, side))

    for ex in (enc, pool, skip):
        ex.wait_sends()
    for row, q, a, missing, wait in (
        (0, 0, 1, top_face, low.wait_above),
        (h + 1, hc + 1, 0, bottom_face, low.wait_below),
    ):

        @pl.when(missing)
        def _():
            x_up[row] = jnp.zeros(x_up.shape[1:], BF16)

        @pl.when(jnp.logical_not(missing))
        def _():
            wait()
            up_rows(q, a, a + 1)

    dec_up_row(0)
    dec_up_row(h - 1)

    low.wait_seams()
    low.load_seams()
    lhs = jnp.concatenate([seam_tmp[3, side, r, 0:8, :] for side in range(2) for r in range(cycles)], axis=0)
    weight = jnp.concatenate([up_w[a, b] for a in range(2) for b in range(2)], axis=1)
    product = jnp.dot(lhs.astype(BF16), weight, preferred_element_type=F32)
    for side in range(2):
        for r in range(cycles):
            code = seam_code[side, r]
            last = lax.rem(code, 2) == 1
            mirrored = code >= 2
            at = 8 * (side * cycles + r)
            phases = []
            for a in range(2):
                pair = [product[at : at + 8, (2 * a + b) * ch : (2 * a + b + 1) * ch] for b in range(2)]
                phases.append(jnp.where(last, pair[1], pair[0]) + up_b[...])
            even = jnp.where(mirrored, phases[1], phases[0])
            odd = jnp.where(mirrored, phases[0], phases[1])
            seam_tmp[4, side, r, 0:1, :] = jnp.where(top_face, 0.0, odd[0:1])
            for k in range(hc):
                seam_tmp[4, side, r, 2 * k + 1 : 2 * k + 2, :] = even[k + 1 : k + 2]
                seam_tmp[4, side, r, 2 * k + 2 : 2 * k + 3, :] = odd[k + 1 : k + 2]
            seam_tmp[4, side, r, h + 1 : h + 2, :] = jnp.where(bottom_face, 0.0, even[hc + 1 : hc + 2])
    for side in range(2):
        pixels[side] = pre[2, side] + terms[side] + seam_term(4, side, dec_side(0, side))
    for side in range(2):
        lo = side * (cols - SUB)
        for r in range(cycles):
            for i in range(h):
                row = pixels[side, 8 * r + i : 8 * r + i + 1, :]
                tile = out[r, i, lo : lo + SUB, :].astype(F32)
                out[r, i, lo : lo + SUB, :] = jnp.where(at_sub == side * (SUB - 1), row, tile).astype(BF16)

    low.wait_sends()


def solution(mesh):
    tiles = mesh.shape["tile"]

    def on_device(fields, seam_tile, seam_code, enc_w, enc_b, mid_w, mid_b, up_w, up_b, dec_w, dec_b):
        cycles, h, cols, ch = fields.shape
        hc = h // 2
        planes = cols // SUB
        cplanes = planes // 2
        vmem = pl.BlockSpec(memory_space=pltpu.VMEM)
        smem = pl.BlockSpec(memory_space=pltpu.SMEM)
        hbm = pl.BlockSpec(memory_space=pl.ANY)
        ends = 2 * cycles
        slots = 2 * FACES
        operands = [
            pltpu.with_memory_space_constraint(x, pltpu.HBM)
            for x in (
                jnp.transpose(seam_tile, (1, 2, 0)).reshape(2, cycles),
                jnp.transpose(seam_code, (1, 2, 0)).reshape(2, cycles),
                fields,
                enc_w,
                mid_w,
                up_w,
                dec_w,
                enc_b.reshape(1, ch),
                mid_b.reshape(1, ch),
                up_b.reshape(1, ch),
                dec_b.reshape(1, ch),
            )
        ]
        return pl.pallas_call(
            functools.partial(kernel, tiles),
            out_shape=jax.ShapeDtypeStruct(fields.shape, BF16),
            in_specs=[smem, smem] + [hbm] * 5 + [vmem] * 4,
            out_specs=vmem,
            scratch_shapes=[
                pltpu.VMEM(fields.shape, BF16),
                pltpu.VMEM(enc_w.shape, BF16),
                pltpu.VMEM(mid_w.shape, BF16),
                pltpu.VMEM(up_w.shape, BF16),
                pltpu.VMEM(dec_w.shape, BF16),
                pltpu.VMEM((h + 2, planes + 2, cycles, SUB, ch), BF16),
                pltpu.VMEM((h + 2, planes + 2, cycles, SUB, ch), BF16),
                pltpu.VMEM((hc + 2, cplanes + 2, cycles, SUB, ch), BF16),
                pltpu.VMEM((h + 2, planes + 2, cycles, SUB, ch), BF16),
                pltpu.VMEM((hc + 2, cplanes, cycles, SUB, ch), BF16),
                pltpu.VMEM((h, planes, cycles, SUB, ch), F32),
                pltpu.VMEM((3, 2, 8 * cycles, ch), F32),
                pltpu.VMEM((2, 8 * cycles, ch), F32),
                pltpu.VMEM((2, 8 * cycles, ch), F32),
                pltpu.VMEM(((planes + 2) * SUB, cols), BF16),
                pltpu.VMEM((cols, cols), BF16),
                pltpu.VMEM((4, ends, 8, ch), F32),
                pltpu.VMEM((4, 2, 8, ch), F32),
                pltpu.VMEM((5, 2, cycles, 16, ch), F32),
                pltpu.VMEM((4, 2, 8, ch), BF16),
                pltpu.VMEM((ends, h, ch), BF16),
                pltpu.VMEM((ends, hc, ch), BF16),
                pltpu.VMEM((ends, h, ch), BF16),
                pltpu.VMEM((ends, hc, ch), BF16),
                pltpu.VMEM((slots, ends, h, ch), BF16),
                pltpu.VMEM((slots, ends, hc, ch), BF16),
                pltpu.VMEM((slots, ends, h, ch), BF16),
                pltpu.VMEM((slots, ends, hc, ch), BF16),
                pltpu.VMEM((2, slots, 8, ch), BF16),
                pltpu.VMEM((2, slots, 8, ch), BF16),
                pltpu.VMEM((2, slots, 8, ch), BF16),
                pltpu.VMEM((2, slots, 8, ch), BF16),
                pltpu.SemaphoreType.DMA((5,)),
                pltpu.SemaphoreType.DMA((4, 6)),
                pltpu.SemaphoreType.DMA((4, 6)),
            ],
            compiler_params=pltpu.CompilerParams(
                collective_id=0, has_side_effects=True, vmem_limit_bytes=44 * 1024 * 1024
            ),
        )(*operands)

    return jax.shard_map(
        on_device,
        mesh=mesh,
        in_specs=(P("grp", "tile", None, None), P(None, "tile", None), P(None, "tile", None)) + (P(),) * 8,
        out_specs=P("grp", "tile", None, None),
        check_vma=False,
    )
```
